768 devices in a mesh: lon: 32 (over y, x_lo, core), lat: 24 (over z, x_hi).
Axes of the slice: x: 4 (x_hi: 2, x_lo: 2; x = x_hi * 2 + x_lo), y: 8, z: 12, core: 2. Of those that a mesh axis runs over, the one named last changes fastest.
Arguments:
- velocity: float32 [2, 1536, 8192], P(None, 'lat', 'lon'), may hold values from -4 to 4
- stress: float32 [3, 1536, 8192], P(None, 'lat', 'lon'), may hold values from -4 to 4
- thickness: float32 [6, 1536, 8192], P(None, 'lat', 'lon'), may hold values from 0.1 to 5
- concentration: float32 [6, 1536, 8192], P(None, 'lat', 'lon'), may hold values from 0.02 to 0.16
- land_mask: int32 [1536, 8192], P('lat', 'lon'), may hold values 0 or 1
- covered: int32 [24, 64], P('lat'), may hold values 0 or 1
- ocean_current: bfloat16 [2, 2, 1536, 8192], P(None, None, 'lat', 'lon'), may hold values from -6 to 6
- wind_stress: bfloat16 [2, 2, 1536, 8192], P(None, None, 'lat', 'lon'), may hold values from -6 to 6
- regrid_weights: bfloat16 [1536, 128], P('lat'), may hold values from -0.5 to 0.5
- tile_offset: int32 [1536], P('lat'), may hold values from -1 to 1, as said below
Outputs:
- velocity_out: float32 [2, 1536, 8192], P(None, 'lat', 'lon')
- stress_out: float32 [3, 1536, 8192], P(None, 'lat', 'lon')
- thickness_out: float32 [6, 1536, 8192], P(None, 'lat', 'lon')
The draws below stay inside these ranges and needn't reach their ends.
Inputs may be any that keep to these rules, and one draw needn't show every extreme that they name: `tile_offset`: never 0; rows of the first tile have +1 and rows of the last tile have -1, so every row reads a tile of the grid.
All inputs are finite; a program needn't handle non-finite values. No bound on the sum of `land_mask` or of `covered` on one device may be relied on, other than what follows from the above.
Results may differ from the reference program's by a relative error of at most 0.0015.
Values may be sent and summed in bfloat16 or wider, within the bound.
A program may use at most 32 MiB of HBM per device.

```python
import math
import jax
import jax.numpy as jnp
from jax import lax

NCAT = 6
CY = 64
BLK = 128
SUB = 4
WIN = 2
NY = 1536
NX = 8192
NT = 24
NBX = 64


def draw_tile_offset(key, part):
    number = jnp.arange(NY)
    picks = 2 * jax.random.randint(key, (NY,), 0, 2) - 1
    return jnp.where(number < CY, 1, jnp.where(number >= NY - CY, -1, picks)).astype(jnp.int32)


def place_ends(result, stream_key, least, high):
    spot = [jax.random.randint(jax.random.fold_in(stream_key, axis), (), 0, length) for axis, length in enumerate(result.shape)]
    main_axis = result.shape.index(max(result.shape))
    beside = spot[:main_axis] + [(spot[main_axis] + 1) % result.shape[main_axis]] + spot[main_axis + 1:]
    return result.at[tuple(spot)].set(least).at[tuple(beside)].set(high)


def block_levels(stream_key, dims, split, least, high):
    factor_of, own = 1.0, jax.random.fold_in(stream_key, 6)
    for position, parts in split:
        draws = jnp.exp(jax.random.uniform(jax.random.fold_in(own, position), (parts,), jnp.float32, least / len(split), high / len(split)))
        factor_of = factor_of * jnp.repeat(draws, dims[position] // parts).reshape([-1 if axis == position else 1 for axis in range(len(dims))])
    return factor_of


def noise(key, shape, deviation, limit, pieces=(), dtype=jnp.bfloat16):
    result = deviation * jax.random.normal(key, shape, jnp.float32)
    if pieces:
        result = result * block_levels(key, shape, pieces, -0.22, 0.18)
    return jnp.clip(result, -limit, limit).astype(dtype)


def setup_inputs(seed: int = 0) -> dict:
    key_list = jax.random.split(jax.random.key(seed), 11)
    return {
        "velocity": noise(key_list[0], (2, NY, NX), 0.5, 4.0, ((1, 24), (2, 32)), jnp.float32),
        "stress": noise(key_list[1], (3, NY, NX), 0.5, 4.0, ((1, 24), (2, 32)), jnp.float32),
        "thickness": jnp.clip(jnp.exp(math.log(5.0) - 3.912023 * jax.random.uniform(key_list[2], (NCAT, NY, NX), jnp.float32) ** block_levels(key_list[2], (NCAT, NY, NX), ((1, 24), (2, 32)), -0.2, 0.2)), 0.1, 5.0),
        "concentration": jnp.clip(0.02 + 0.14 * jax.random.uniform(key_list[3], (NCAT, NY, NX), jnp.float32) ** block_levels(key_list[3], (NCAT, NY, NX), ((1, 24), (2, 32)), -0.2, 0.2), 0.02, 0.16),
        "land_mask": place_ends((jax.random.randint(key_list[4], (NY, NX), 0, 8) < 7).astype(jnp.int32), jax.random.fold_in(key_list[4], 1), 0, 1),
        "covered": place_ends((jax.random.randint(key_list[5], (NT, NBX), 0, 2) < 1).astype(jnp.int32), jax.random.fold_in(key_list[5], 1), 0, 1),
        "ocean_current": noise(key_list[6], (WIN, 2, NY, NX), 1.0, 6.0, ((2, 24), (3, 32))),
        "wind_stress": noise(key_list[7], (WIN, 2, NY, NX), 1.0, 6.0, ((2, 24), (3, 32))),
        "regrid_weights": noise(key_list[8], (NY, 2 * CY), (2 * CY) ** -0.5, 0.5, ((0, 24),)),
        "tile_offset": draw_tile_offset(jax.random.fold_in(key_list[10], 71), 0),
    }


relax_rate = 0.5
strain_offset = 0.5
time_step = 0.5
water_drag = 1.0
growth_rate = 0.3
mixing_rate = 0.3

def toward_east(field):
    return jnp.roll(field, -1, axis=-1)

def toward_west(field):
    return jnp.roll(field, 1, axis=-1)

def toward_north(field):
    zero_row = jnp.zeros_like(field[..., :1, :])
    return jnp.concatenate([field[..., 1:, :], zero_row], axis=-2)

def toward_south(field):
    zero_row = jnp.zeros_like(field[..., :1, :])
    return jnp.concatenate([zero_row, field[..., :-1, :]], axis=-2)

def growth(thick_now, conc_now):
    ice_area = lax.optimization_barrier(jnp.sum(conc_now, axis=0))
    mean_thick = lax.optimization_barrier(jnp.sum(conc_now * thick_now, axis=0)) / ice_area
    return thick_now + growth_rate / (0.5 + thick_now) + mixing_rate * (mean_thick - thick_now)

def forcing(thick_now, conc_now):
    volume = lax.optimization_barrier(jnp.sum(conc_now * thick_now, axis=0))
    ice_area = lax.optimization_barrier(jnp.sum(conc_now, axis=0))
    strength = volume * jnp.exp(-2.0 * (1.0 - ice_area))
    return (strength, volume + 0.5)

def new_stress(east_u, west_u, north_u, south_u, east_v, west_v, north_v, south_v, stresses, strength, open_mask):
    stretch_x = (east_u - west_u) / 2.0
    stretch_y = (north_v - south_v) / 2.0
    shear_half = (north_u - south_u + (east_v - west_v)) / 4.0
    divergence = stretch_x + stretch_y
    tension = stretch_x - stretch_y
    shearing = 2.0 * shear_half
    deformation = jnp.sqrt(divergence * divergence + (tension * tension + shearing * shearing) / 4.0 + strain_offset * strain_offset)
    bulk_stress = (stresses[0] + relax_rate * strength * (divergence / deformation - 1.0)) / (1.0 + relax_rate) * open_mask
    tension_stress = (stresses[1] + relax_rate * strength * tension / (4.0 * deformation)) / (1.0 + relax_rate) * open_mask
    shear_stress = (stresses[2] + relax_rate * strength * shearing / (8.0 * deformation)) / (1.0 + relax_rate) * open_mask
    return jnp.stack([bulk_stress, tension_stress, shear_stress])

def new_velocity(sxx_east, sxx_west, syy_north, syy_south, sxy_east, sxy_west, sxy_north, sxy_south, velocity_now, ice_mass, current, wind_now, open_mask):
    force_x = (sxx_east - sxx_west) / 2.0 + (sxy_north - sxy_south) / 2.0
    force_y = (sxy_east - sxy_west) / 2.0 + (syy_north - syy_south) / 2.0
    damping = 1.0 + time_step * water_drag / ice_mass
    u = (velocity_now[0] + time_step * (force_x + wind_now[0] + water_drag * current[0]) / ice_mass) / damping * open_mask
    v = (velocity_now[1] + time_step * (force_y + wind_now[1] + water_drag * current[1]) / ice_mass) / damping * open_mask
    return jnp.stack([u, v])

def reference(velocity, stress, thickness, concentration, land_mask, covered, ocean_current, wind_stress, regrid_weights, tile_offset):
    open_mask = land_mask.astype(jnp.float32)
    covered_cells = jnp.repeat(jnp.repeat(covered, CY, axis=0), BLK, axis=1) > 0
    ocean_tiles = ocean_current.astype(jnp.float32).reshape(WIN, 2, NT, CY, NX)
    numbers = jnp.arange(NT).astype(jnp.int32)
    upper_index = jnp.clip(numbers + 1, 0, NT - 1).astype(jnp.int32)
    lower_index = jnp.clip(numbers - 1, 0, NT - 1).astype(jnp.int32)
    upper_tiles = jnp.take(ocean_tiles, upper_index, axis=2)
    lower_tiles = jnp.take(ocean_tiles, lower_index, axis=2)
    weights = regrid_weights.astype(jnp.float32).reshape(NT, CY, 2 * CY)
    currents = jnp.einsum('tij,wctjx->wctix', weights[:, :, :CY], ocean_tiles, precision=lax.Precision.HIGHEST)
    from_upper = jnp.einsum('tij,wctjx->wctix', weights[:, :, CY:], upper_tiles, precision=lax.Precision.HIGHEST)
    from_lower = jnp.einsum('tij,wctjx->wctix', weights[:, :, CY:], lower_tiles, precision=lax.Precision.HIGHEST)
    upward = (tile_offset.reshape(NT, CY) > 0)[None, None, :, :, None]
    currents = currents + jnp.where(upward, from_upper, from_lower)
    currents = currents.reshape(WIN, 2, NY, NX)
    thick_now = thickness
    velocity_now = velocity
    stresses = stress
    for window in range(WIN):
        thick_now = jnp.where(covered_cells, growth(thick_now, concentration), thick_now)
        strength, ice_mass = forcing(thick_now, concentration)
        wind_now = wind_stress[window].astype(jnp.float32)
        current = currents[window]
        for substep in range(SUB):
            u = velocity_now[0]
            v = velocity_now[1]
            stresses = new_stress(toward_east(u), toward_west(u), toward_north(u), toward_south(u), toward_east(v), toward_west(v), toward_north(v), toward_south(v), stresses, strength, open_mask)
            sigma_xx = (stresses[0] + stresses[1]) / 2.0
            sigma_yy = (stresses[0] - stresses[1]) / 2.0
            sigma_xy = stresses[2]
            velocity_now = new_velocity(toward_east(sigma_xx), toward_west(sigma_xx), toward_north(sigma_yy), toward_south(sigma_yy), toward_east(sigma_xy), toward_west(sigma_xy), toward_north(sigma_xy), toward_south(sigma_xy), velocity_now, ice_mass, current, wind_now, open_mask)
    return (velocity_now, stresses, thick_now)
```

```python
import jax
import jax.numpy as jnp
from jax import lax
from jax.experimental import pallas as pl
from jax.experimental.pallas import tpu as pltpu
from jax.sharding import PartitionSpec as P

MESH = pl.DeviceIdType.MESH
F32 = jnp.float32
BF16 = jnp.bfloat16

ROWS = 64
LANES = 128
DEEP = 16
PAD = 8
BASE = PAD + DEEP
TALL = ROWS + 2 * BASE
SUB = 4
CATS = 6

U, V, X, Y, S, B0, E0, B1, E1, GX0, GY0, GX1, GY1 = range(13)
STATE = ((U,), (V,), (X,), (Y,), (S,), (B0,), (E0,), (B1, E1))
FORCE0 = ((GX0,), (GY0,))
FORCE1 = ((GX1, GY1),)


def lane_ids(rows):
    return lax.broadcasted_iota(jnp.int32, (rows, LANES), 1)


def turn(value, shift):
    shift = shift % LANES
    return pltpu.roll(value, shift, 1) if shift else value


def pack_sides(ext, rim, edge, blocks):
    top, low = BASE + ROWS - DEEP, BASE
    for k, block in enumerate(blocks):
        for c in range(2):
            if len(block) == 1:
                rim[0, k, c] = ext[block[0], c, top : top + DEEP, :].astype(BF16)
                rim[1, k, c] = ext[block[0], c, low : low + DEEP, :].astype(BF16)
            else:
                one, two = block
                half = DEEP // 2
                rim[0, k, c] = jnp.concatenate(
                    [ext[one, c, top + half : top + DEEP, :], ext[two, c, top + half : top + DEEP, :]], axis=0
                ).astype(BF16)
                rim[1, k, c] = jnp.concatenate(
                    [ext[one, c, low : low + half, :], ext[two, c, low : low + half, :]], axis=0
                ).astype(BF16)
    lanes = lane_ids(DEEP)
    for piece in range(ROWS // DEEP):
        rows = slice(BASE + piece * DEEP, BASE + (piece + 1) * DEEP)
        east = jnp.zeros((DEEP, LANES), F32)
        west = jnp.zeros((DEEP, LANES), F32)
        for k, block in enumerate(blocks):
            width = DEEP // len(block)
            for part, field in enumerate(block):
                start = DEEP * k + width * part
                here = (lanes >= start) & (lanes < start + width)
                east = jnp.where(here, turn(ext[field, 1, rows, :], start - (LANES - width)), east)
                west = jnp.where(here, turn(ext[field, 0, rows, :], start), west)
        edge[0, piece * DEEP : (piece + 1) * DEEP, :] = east.astype(BF16)
        edge[1, piece * DEEP : (piece + 1) * DEEP, :] = west.astype(BF16)


def unpack_sides(ext, rim, edge, blocks, north_in, south_in):
    for k, block in enumerate(blocks):
        for c in range(2):
            from_north = rim[0, k, c].astype(F32) * north_in
            from_south = rim[1, k, c].astype(F32) * south_in
            top, low = BASE + ROWS, BASE - DEEP
            if len(block) == 1:
                ext[block[0], c, top : top + DEEP, :] = from_north
                ext[block[0], c, low : low + DEEP, :] = from_south
            else:
                half = DEEP // 2
                for part, field in enumerate(block):
                    ext[field, c, top : top + half, :] = from_north[part * half : (part + 1) * half]
                    ext[field, c, low + half : low + DEEP, :] = from_south[part * half : (part + 1) * half]
    left = lane_ids(DEEP) < LANES // 2
    pieces = ROWS // DEEP + 2
    for piece in range(pieces):
        rows = slice(piece * DEEP, (piece + 1) * DEEP)
        east = edge[0, rows, :].astype(F32)
        west = edge[1, rows, :].astype(F32)
        if piece == 0:
            east, west = east * south_in, west * south_in
        if piece == pieces - 1:
            east, west = east * north_in, west * north_in
        for k, block in enumerate(blocks):
            width = DEEP // len(block)
            for part, field in enumerate(block):
                start = DEEP * k + width * part
                ext[field, 2, PAD + piece * DEEP : PAD + (piece + 1) * DEEP, :] = jnp.where(
                    left, turn(east, -start), turn(west, LANES - width - start)
                )


def side_copies(rim_out, edge_out, rim_in, edge_in, send, recv, lat, lon, lats, lons):
    north, south = lax.rem(lat + 1, lats), lax.rem(lat + lats - 1, lats)
    east, west = lax.rem(lon + 1, lons), lax.rem(lon + lons - 1, lons)
    tail, end = pl.ds(ROWS - DEEP, DEEP), pl.ds(ROWS + DEEP, DEEP)
    head, body = pl.ds(0, DEEP), pl.ds(DEEP, ROWS)
    plan = (
        (rim_out.at[0], rim_in.at[1], north, lon),
        (rim_out.at[1], rim_in.at[0], south, lon),
        (edge_out.at[0], edge_in.at[1, body], lat, east),
        (edge_out.at[1], edge_in.at[0, body], lat, west),
        (edge_out.at[0, tail], edge_in.at[1, head], north, east),
        (edge_out.at[1, tail], edge_in.at[0, head], north, west),
        (edge_out.at[0, head], edge_in.at[1, end], south, east),
        (edge_out.at[1, head], edge_in.at[0, end], south, west),
    )
    return [
        pltpu.make_async_remote_copy(
            src_ref=source,
            dst_ref=target,
            send_sem=send.at[i],
            recv_sem=recv.at[i],
            device_id={"lat": to_lat, "lon": to_lon},
            device_id_type=MESH,
        )
        for i, (source, target, to_lat, to_lon) in enumerate(plan)
    ]


def spread(tiles, first, last):
    ahead = [turn(t, -1) for t in tiles]
    behind = [turn(t, 1) for t in tiles]
    return [
        jnp.where(last, ahead[(c + 1) % 3], ahead[c]) - jnp.where(first, behind[(c + 2) % 3], behind[c])
        for c in range(3)
    ]


def stress_rows(ext, row, bulk, mass, first, last):
    def at(field, shift):
        return [ext[field, c, pl.ds(row + shift, 8), :] for c in range(3)]

    du = spread(at(U, 0), first, last)
    dv = spread(at(V, 0), first, last)
    un, us, vn, vs = at(U, 1), at(U, -1), at(V, 1), at(V, -1)
    for c in range(3):
        rows = pl.ds(row, 8)
        up = vn[c] - vs[c]
        shear = (un[c] - us[c]) + dv[c]
        div = du[c] + up
        ten = du[c] - up
        rate = lax.rsqrt(div * div + 0.25 * (ten * ten + shear * shear) + 1.0)
        b = ext[bulk, c, rows, :]
        keep = jnp.where(ext[mass, c, rows, :] > 0.0, 2.0 / 3.0, 0.0)
        br = b * rate
        quarter = 0.25 * br
        press = br * div - b
        pull = quarter * ten
        ext[X, c, rows, :] = (keep * ext[X, c, rows, :] + press) + pull
        ext[Y, c, rows, :] = (keep * ext[Y, c, rows, :] + press) - pull
        ext[S, c, rows, :] = keep * ext[S, c, rows, :] + quarter * shear


def velocity_rows(ext, row, mass, gx, gy, first, last):
    def at(field, shift):
        return [ext[field, c, pl.ds(row + shift, 8), :] for c in range(3)]

    dx = spread(at(X, 0), first, last)
    ds = spread(at(S, 0), first, last)
    yn, ys, sn, ss = at(Y, 1), at(Y, -1), at(S, 1), at(S, -1)
    for c in range(3):
        rows = pl.ds(row, 8)
        e = ext[mass, c, rows, :]
        keep = jnp.where(e > 0.0, 1.0 - e, 0.0)
        fx = dx[c] + (sn[c] - ss[c])
        fy = ds[c] + (yn[c] - ys[c])
        ext[U, c, rows, :] = keep * ext[U, c, rows, :] + (ext[gx, c, rows, :] + e * fx)
        ext[V, c, rows, :] = keep * ext[V, c, rows, :] + (ext[gy, c, rows, :] + e * fy)


def tiles_within(reach):
    above = (reach + 7) // 8
    return BASE // 8 - above, BASE // 8 + ROWS // 8 + above


def sweep(low, high, body):
    def step(i, carry):
        body(pl.multiple_of(i * 8, 8))
        return carry

    lax.fori_loop(low, high, step, 0)


def kernel(
    vel_hbm,
    str_hbm,
    thk_hbm,
    con_hbm,
    land_hbm,
    cov_hbm,
    oce_hbm,
    win_hbm,
    reg_hbm,
    off_hbm,
    vel_out,
    str_out,
    thk_out,
    vel,
    stress,
    thk,
    con,
    land,
    cov,
    oce,
    win,
    reg,
    off,
    ext,
    rim_a_out,
    edge_a_out,
    rim_a_in,
    edge_a_in,
    rim_b_out,
    edge_b_out,
    rim_b_in,
    edge_b_in,
    rim_c_out,
    edge_c_out,
    rim_c_in,
    edge_c_in,
    load_sem,
    send_a,
    recv_a,
    send_b,
    recv_b,
    send_c,
    recv_c,
    send_o,
    recv_o,
):
    lat, lon = lax.axis_index("lat"), lax.axis_index("lon")
    lats, lons = lax.axis_size("lat"), lax.axis_size("lon")
    north, south = lax.rem(lat + 1, lats), lax.rem(lat + lats - 1, lats)
    east, west = lax.rem(lon + 1, lons), lax.rem(lon + lons - 1, lons)

    barrier = pltpu.get_barrier_semaphore()
    around = ((north, lon), (south, lon), (lat, east), (lat, west), (north, east), (north, west), (south, east), (south, west))
    for to_lat, to_lon in around:
        pl.semaphore_signal(barrier, inc=1, device_id={"lat": to_lat, "lon": to_lon}, device_id_type=MESH)

    loads = [
        pltpu.make_async_copy(source, target, load_sem.at[i])
        for i, (source, target) in enumerate(
            (
                (vel_hbm, vel),
                (str_hbm, stress),
                (thk_hbm, thk),
                (con_hbm, con),
                (land_hbm, land),
                (cov_hbm, cov),
                (win_hbm, win),
                (reg_hbm, reg),
                (off_hbm, off),
                (oce_hbm, oce.at[:, :, pl.ds(0, ROWS), :]),
            )
        )
    ]
    for load in loads:
        load.start()
    ocean = []
    for w in range(2):
        for d, (target, slot) in enumerate(((north, 2), (south, 1))):
            ocean.append(
                pltpu.make_async_remote_copy(
                    src_ref=oce_hbm.at[w],
                    dst_ref=oce.at[w, :, pl.ds(slot * ROWS, ROWS), :],
                    send_sem=send_o.at[2 * w + d],
                    recv_sem=recv_o.at[2 * w + d],
                    device_id={"lat": target, "lon": lon},
                    device_id_type=MESH,
                )
            )
    pl.semaphore_wait(barrier, len(around))
    ocean[0].start()
    ocean[1].start()

    for load in loads[:6]:
        load.wait()

    lanes_one = lane_ids(1)[:, : cov.shape[1]]
    flags = [
        jnp.sum(jnp.where(lanes_one == 2 * lon + c, cov[...], 0), axis=1, keepdims=True) > 0 for c in range(2)
    ]

    def prepare(i, carry):
        row = pl.multiple_of(i * 8, 8)
        rows = pl.ds(row, 8)
        inner = pl.ds(pl.multiple_of(BASE + row, 8), 8)
        for c in range(2):
            cells = slice(c * LANES, (c + 1) * LANES)
            ext[U, c, inner, :] = vel[0, rows, cells]
            ext[V, c, inner, :] = vel[1, rows, cells]
            one, two = stress[0, rows, cells], stress[1, rows, cells]
            ext[X, c, inner, :] = 0.25 * (one + two)
            ext[Y, c, inner, :] = 0.25 * (one - two)
            ext[S, c, inner, :] = 0.5 * stress[2, rows, cells]
            open_mask = land[rows, cells].astype(F32)
            share = [con[k, rows, cells] for k in range(CATS)]
            thick = [thk[k, rows, cells] for k in range(CATS)]
            area = sum(share[1:], share[0])
            weight = jnp.exp(-2.0 * (1.0 - area)) * open_mask * (1.0 / 12.0)
            volume = sum((share[k] * thick[k] for k in range(1, CATS)), share[0] * thick[0])
            grow = jnp.broadcast_to(flags[c], (8, LANES))
            for bulk, mass in ((B0, E0), (B1, E1)):
                mean = volume / area
                thick = [jnp.where(grow, t + 0.3 / (0.5 + t) + 0.3 * (mean - t), t) for t in thick]
                volume = sum((share[k] * thick[k] for k in range(1, CATS)), share[0] * thick[0])
                ext[bulk, c, inner, :] = volume * weight
                ext[mass, c, inner, :] = 0.5 * open_mask / (volume + 1.0)
            for k in range(CATS):
                thk_out[k, rows, cells] = thick[k]
        return carry

    lax.fori_loop(0, ROWS // 8, prepare, 0)

    pack_sides(ext, rim_a_out, edge_a_out, STATE)
    copies_a = side_copies(rim_a_out, edge_a_out, rim_a_in, edge_a_in, send_a, recv_a, lat, lon, lats, lons)
    for copy in copies_a:
        copy.start()
    ocean[2].start()
    ocean[3].start()

    for load in loads[6:]:
        load.wait()
    line = lax.broadcasted_iota(jnp.int32, (ROWS, ROWS), 0)
    mark = lax.broadcasted_iota(jnp.int32, (ROWS, ROWS), 1)
    upward = jnp.sum(jnp.where(line == mark, jnp.broadcast_to(off[...], (ROWS, ROWS)), 0), axis=1, keepdims=True) > 0
    upward = jnp.broadcast_to(upward, (ROWS, LANES))
    weights = reg[...].astype(F32)
    high = jnp.where((lane_ids(ROWS) < ROWS) | upward, weights, 0.0).astype(BF16)
    deep = jnp.where(upward, 0.0, turn(weights, ROWS)).astype(BF16)[:, :ROWS]

    def force(w, mass, fields):
        for part, field in enumerate(fields):
            current = jnp.dot(high, oce[w, part, : 2 * ROWS, :], preferred_element_type=F32)
            current = current + jnp.dot(deep, oce[w, part, 2 * ROWS :, :], preferred_element_type=F32)
            total = current + win[w, part].astype(F32)
            for c in range(2):
                inner = slice(BASE, BASE + ROWS)
                ext[field, c, inner, :] = ext[mass, c, inner, :] * total[:, c * LANES : (c + 1) * LANES]

    north_in = jnp.where(lat == lats - 1, 0.0, 1.0).astype(F32)
    south_in = jnp.where(lat == 0, 0.0, 1.0).astype(F32)

    ocean[0].wait_recv()
    ocean[1].wait_recv()
    force(0, E0, (GX0, GY0))
    pack_sides(ext, rim_b_out, edge_b_out, FORCE0)
    copies_b = side_copies(rim_b_out, edge_b_out, rim_b_in, edge_b_in, send_b, recv_b, lat, lon, lats, lons)
    for copy in copies_b:
        copy.start()

    for copy in copies_a:
        copy.wait_recv()
    unpack_sides(ext, rim_a_in, edge_a_in, STATE, north_in, south_in)

    ocean[2].wait_recv()
    ocean[3].wait_recv()
    force(1, E1, (GX1, GY1))
    pack_sides(ext, rim_c_out, edge_c_out, FORCE1)
    copies_c = side_copies(rim_c_out, edge_c_out, rim_c_in, edge_c_in, send_c, recv_c, lat, lon, lats, lons)
    for copy in copies_c:
        copy.start()

    lanes = lane_ids(8)
    first, last = lanes == 0, lanes == LANES - 1
    settings = ((B0, E0, GX0, GY0, copies_b, rim_b_in, edge_b_in, FORCE0), (B1, E1, GX1, GY1, copies_c, rim_c_in, edge_c_in, FORCE1))
    reach = DEEP
    for bulk, mass, gx, gy, copies, rim_in, edge_in, blocks in settings:
        for step in range(SUB):
            low, high_row = tiles_within(reach - 1)
            sweep(low, high_row, lambda row: stress_rows(ext, row, bulk, mass, first, last))
            if step == 0:
                for copy in copies:
                    copy.wait_recv()
                unpack_sides(ext, rim_in, edge_in, blocks, north_in, south_in)
            low, high_row = tiles_within(reach - 2)
            sweep(low, high_row, lambda row: velocity_rows(ext, row, mass, gx, gy, first, last))
            reach -= 2

    for c in range(2):
        cells = slice(c * LANES, (c + 1) * LANES)
        inner = slice(BASE, BASE + ROWS)
        vel_out[0, :, cells] = ext[U, c, inner, :]
        vel_out[1, :, cells] = ext[V, c, inner, :]
        one, two = ext[X, c, inner, :], ext[Y, c, inner, :]
        str_out[0, :, cells] = 2.0 * (one + two)
        str_out[1, :, cells] = 2.0 * (one - two)
        str_out[2, :, cells] = 2.0 * ext[S, c, inner, :]

    for copy in ocean + copies_a + copies_b + copies_c:
        copy.wait_send()


def local(velocity, stress, thickness, concentration, land_mask, covered, ocean_current, wind_stress, regrid_weights, tile_offset):
    offsets = tile_offset.reshape(1, -1)
    arrays = (velocity, stress, thickness, concentration, land_mask, covered, ocean_current, wind_stress, regrid_weights, offsets)
    width = velocity.shape[-1]
    ocean_rows = (2, 2, 3 * ROWS, width)

    def rim(blocks):
        return pltpu.VMEM((2, len(blocks), 2, DEEP, LANES), BF16)

    edge_out = pltpu.VMEM((2, ROWS, LANES), BF16)
    edge_in = pltpu.VMEM((2, ROWS + 2 * DEEP, LANES), BF16)
    staged = [
        pltpu.VMEM(ocean_rows if i == 6 else a.shape, a.dtype) for i, a in enumerate(arrays)
    ]
    sides = [item for blocks in (STATE, FORCE0, FORCE1) for item in (rim(blocks), edge_out, rim(blocks), edge_in)]
    dma = pltpu.SemaphoreType.DMA
    return pl.pallas_call(
        kernel,
        out_shape=(
            jax.ShapeDtypeStruct(velocity.shape, F32),
            jax.ShapeDtypeStruct(stress.shape, F32),
            jax.ShapeDtypeStruct(thickness.shape, F32),
        ),
        in_specs=[pl.BlockSpec(memory_space=pl.ANY)] * len(arrays),
        out_specs=[pl.BlockSpec(memory_space=pltpu.VMEM)] * 3,
        scratch_shapes=staged
        + [pltpu.VMEM((13, 3, TALL, LANES), F32)]
        + sides
        + [dma((10,)), dma((8,)), dma((8,)), dma((8,)), dma((8,)), dma((8,)), dma((8,)), dma((4,)), dma((4,))],
        compiler_params=pltpu.CompilerParams(collective_id=0, has_side_effects=True),
    )(*arrays)


def solution(mesh):
    return jax.shard_map(
        local,
        mesh=mesh,
        in_specs=(
            P(None, "lat", "lon"),
            P(None, "lat", "lon"),
            P(None, "lat", "lon"),
            P(None, "lat", "lon"),
            P("lat", "lon"),
            P("lat", None),
            P(None, None, "lat", "lon"),
            P(None, None, "lat", "lon"),
            P("lat", None),
            P("lat"),
        ),
        out_specs=(P(None, "lat", "lon"), P(None, "lat", "lon"), P(None, "lat", "lon")),
        check_vma=False,
    )
```

```python
import jax
import jax.numpy as jnp
from jax import lax
from jax.experimental import pallas as pl
from jax.experimental.pallas import tpu as pltpu
from jax.sharding import PartitionSpec as P

MESH = pl.DeviceIdType.MESH
F32 = jnp.float32
BF16 = jnp.bfloat16

ROWS = 64
LANES = 128
DEEP = 16
PAD = 8
BASE = PAD + DEEP
TALL = ROWS + 2 * BASE
SUB = 4
CATS = 6

U, V, X, Y, S, B0, E0, B1, E1, GX0, GY0, GX1, GY1 = range(13)
STATE = ((U,), (V,), (X,), (Y,), (S,), (B0,), (E0,), (B1, E1))
WIDE = ROWS + 2 * DEEP
NEAR = (-2, -1, 0, 1, 2)
GROUP = 2


def lane_ids(rows):
    return lax.broadcasted_iota(jnp.int32, (rows, LANES), 1)


def turn(value, shift):
    shift = shift % LANES
    return pltpu.roll(value, shift, 1) if shift else value


def pack_sides(ext, rim, edge):
    top, low = BASE + ROWS - DEEP, BASE
    half = DEEP // 2
    for k, block in enumerate(STATE):
        for c in range(2):
            if len(block) == 1:
                rim[0, k, c] = ext[block[0]][c, top : top + DEEP, :].astype(BF16)
                rim[1, k, c] = ext[block[0]][c, low : low + DEEP, :].astype(BF16)
            else:
                one, two = ext[block[0]], ext[block[1]]
                rim[0, k, c] = jnp.concatenate([one[c, top + half : top + DEEP, :], two[c, top + half : top + DEEP, :]], axis=0).astype(BF16)
                rim[1, k, c] = jnp.concatenate([one[c, low : low + half, :], two[c, low : low + half, :]], axis=0).astype(BF16)
    lanes = lane_ids(DEEP)
    for piece in range(ROWS // DEEP):
        rows = slice(BASE + piece * DEEP, BASE + (piece + 1) * DEEP)
        east = jnp.zeros((DEEP, LANES), F32)
        west = jnp.zeros((DEEP, LANES), F32)
        for k, block in enumerate(STATE):
            width = DEEP // len(block)
            for part, field in enumerate(block):
                start = DEEP * k + width * part
                here = (lanes >= start) & (lanes < start + width)
                east = jnp.where(here, turn(ext[field][1, rows, :], start - (LANES - width)), east)
                west = jnp.where(here, turn(ext[field][0, rows, :], start), west)
        edge[0, piece * DEEP : (piece + 1) * DEEP, :] = east.astype(BF16)
        edge[1, piece * DEEP : (piece + 1) * DEEP, :] = west.astype(BF16)


def unpack_sides(ext, rim, edge, north_in, south_in):
    half = DEEP // 2
    top, low = BASE + ROWS, BASE - DEEP
    for k, block in enumerate(STATE):
        for c in range(2):
            from_north = rim[0, k, c].astype(F32) * north_in
            from_south = rim[1, k, c].astype(F32) * south_in
            if len(block) == 1:
                ext[block[0]][c, top : top + DEEP, :] = from_north
                ext[block[0]][c, low : low + DEEP, :] = from_south
            else:
                for part, field in enumerate(block):
                    ext[field][c, top : top + half, :] = from_north[part * half : (part + 1) * half]
                    ext[field][c, low + half : low + DEEP, :] = from_south[part * half : (part + 1) * half]
    left = lane_ids(DEEP) < LANES // 2
    pieces = WIDE // DEEP
    for piece in range(pieces):
        rows = slice(piece * DEEP, (piece + 1) * DEEP)
        east = edge[0, rows, :].astype(F32)
        west = edge[1, rows, :].astype(F32)
        if piece == 0:
            east, west = east * south_in, west * south_in
        if piece == pieces - 1:
            east, west = east * north_in, west * north_in
        for k, block in enumerate(STATE):
            width = DEEP // len(block)
            for part, field in enumerate(block):
                start = DEEP * k + width * part
                ext[field][2, PAD + piece * DEEP : PAD + (piece + 1) * DEEP, :] = jnp.where(
                    left, turn(east, -start), turn(west, LANES - width - start)
                )


def pack_ocean(ocean, wind, side):
    lanes = lane_ids(ROWS)
    east = jnp.zeros((ROWS, LANES), F32)
    west = jnp.zeros((ROWS, LANES), F32)
    for k in range(8):
        w, part = (k % 4) // 2, k % 2
        if k < 4:
            field = ocean[w, part, 2 * ROWS : 3 * ROWS, :]
        else:
            field = wind[w, part, DEEP : DEEP + ROWS, :]
        start = DEEP * k
        here = (lanes >= start) & (lanes < start + DEEP)
        east = jnp.where(here, turn(field[:, LANES:].astype(F32), start + DEEP), east)
        west = jnp.where(here, turn(field[:, :LANES].astype(F32), start), west)
    side[0] = east.astype(BF16)
    side[1] = west.astype(BF16)


def spread(tiles, first, last):
    ahead = [turn(t, -1) for t in tiles]
    behind = [turn(t, 1) for t in tiles]
    return [
        jnp.where(last, ahead[(c + 1) % 3], ahead[c]) - jnp.where(first, behind[(c + 2) % 3], behind[c])
        for c in range(3)
    ]


def stress_rows(ext, rows_list, bulk, mass, first, last):
    results = []
    for row in rows_list:

        def at(field, shift):
            return [ext[field][c, pl.ds(row + shift, 8), :] for c in range(3)]

        du = spread(at(U, 0), first, last)
        dv = spread(at(V, 0), first, last)
        un, us, vn, vs = at(U, 1), at(U, -1), at(V, 1), at(V, -1)
        bs, es, xs, ys, ss = at(bulk, 0), at(mass, 0), at(X, 0), at(Y, 0), at(S, 0)
        for c in range(3):
            up = vn[c] - vs[c]
            shear = (un[c] - us[c]) + dv[c]
            div = du[c] + up
            ten = du[c] - up
            rate = lax.rsqrt(div * div + 0.25 * (ten * ten + shear * shear) + 1.0)
            keep = jnp.where(es[c] > 0.0, 2.0 / 3.0, 0.0)
            br = bs[c] * rate
            quarter = 0.25 * br
            press = br * div - bs[c]
            pull = quarter * ten
            common = keep * xs[c] + press
            other = keep * ys[c] + press
            results.append((row, c, common + pull, other - pull, keep * ss[c] + quarter * shear))
    for row, c, x, y, s in results:
        rows = pl.ds(row, 8)
        ext[X][c, rows, :] = x
        ext[Y][c, rows, :] = y
        ext[S][c, rows, :] = s


def velocity_rows(ext, rows_list, mass, gx, gy, first, last):
    results = []
    for row in rows_list:

        def at(field, shift):
            return [ext[field][c, pl.ds(row + shift, 8), :] for c in range(3)]

        dx = spread(at(X, 0), first, last)
        ds = spread(at(S, 0), first, last)
        yn, ys, sn, ss = at(Y, 1), at(Y, -1), at(S, 1), at(S, -1)
        es, us, vs, gxs, gys = at(mass, 0), at(U, 0), at(V, 0), at(gx, 0), at(gy, 0)
        for c in range(3):
            e = es[c]
            keep = jnp.where(e > 0.0, 1.0 - e, 0.0)
            fx = dx[c] + (sn[c] - ss[c])
            fy = ds[c] + (yn[c] - ys[c])
            results.append((row, c, keep * us[c] + (gxs[c] + e * fx), keep * vs[c] + (gys[c] + e * fy)))
    for row, c, u, v in results:
        rows = pl.ds(row, 8)
        ext[U][c, rows, :] = u
        ext[V][c, rows, :] = v


def tiles_within(reach):
    above = (reach + 7) // 8
    return BASE // 8 - above, BASE // 8 + ROWS // 8 + above


def sweep(low, high, body):
    def step(i, carry):
        start = pl.multiple_of((low + i * GROUP) * 8, 8)
        body([start + 8 * j for j in range(GROUP)])
        return carry

    lax.fori_loop(0, (high - low) // GROUP, step, 0)


def kernel(
    vel_hbm,
    str_hbm,
    thk_hbm,
    con_hbm,
    land_hbm,
    cov_hbm,
    oce_hbm,
    win_hbm,
    reg_hbm,
    off_hbm,
    vel_out,
    str_out,
    thk_out,
    vel,
    stress,
    thk,
    con,
    land,
    cov,
    oce,
    win,
    reg,
    off,
    u_ref,
    v_ref,
    x_ref,
    y_ref,
    s_ref,
    b0_ref,
    e0_ref,
    b1_ref,
    e1_ref,
    gx0_ref,
    gy0_ref,
    gx1_ref,
    gy1_ref,
    rim_out,
    edge_out,
    rim_in,
    edge_in,
    side_out,
    side_in,
    mix_out,
    mix_in,
    mix,
    load_sem,
    send_a,
    recv_a,
    send_o,
    recv_o,
    send_s,
    recv_s,
    send_m,
    recv_m,
):
    ext = (u_ref, v_ref, x_ref, y_ref, s_ref, b0_ref, e0_ref, b1_ref, e1_ref, gx0_ref, gy0_ref, gx1_ref, gy1_ref)
    lat, lon = lax.axis_index("lat"), lax.axis_index("lon")
    lats, lons = lax.axis_size("lat"), lax.axis_size("lon")

    def place(up, right):
        return lax.rem(lat + lats + up, lats), lax.rem(lon + lons + right, lons)

    def send_to(up, right, source, target, send, recv):
        to_lat, to_lon = place(up, right)
        return pltpu.make_async_remote_copy(
            src_ref=source,
            dst_ref=target,
            send_sem=send,
            recv_sem=recv,
            device_id={"lat": to_lat, "lon": to_lon},
            device_id_type=MESH,
        )

    barrier = pltpu.get_barrier_semaphore()
    around = [(up, right) for up in NEAR for right in (-1, 0, 1) if up or right]
    for up, right in around:
        to_lat, to_lon = place(up, right)
        pl.semaphore_signal(barrier, inc=1, device_id={"lat": to_lat, "lon": to_lon}, device_id_type=MESH)

    own = pl.ds(2 * ROWS, ROWS)
    loads = [
        pltpu.make_async_copy(source, target, load_sem.at[i])
        for i, (source, target) in enumerate(
            (
                (oce_hbm, oce.at[:, :, own, :]),
                (win_hbm, win.at[:, :, pl.ds(DEEP, ROWS), :]),
                (reg_hbm, reg),
                (off_hbm, off),
                (thk_hbm, thk),
                (con_hbm, con),
                (land_hbm, land),
                (cov_hbm, cov),
                (vel_hbm, vel),
                (str_hbm, stress),
            )
        )
    ]
    for load in loads:
        load.start()

    tail, head = pl.ds(ROWS - DEEP, DEEP), pl.ds(0, DEEP)
    ocean = [
        [
            send_to(
                up,
                0,
                oce_hbm.at[w],
                oce.at[w, :, pl.ds((2 - up) * ROWS, ROWS), :],
                send_o.at[4 * w + i],
                recv_o.at[4 * w + i],
            )
            for i, up in enumerate((1, -1, 2, -2))
        ]
        for w in range(2)
    ]
    winds = [
        send_to(1, 0, win_hbm.at[:, :, tail, :], win.at[:, :, pl.ds(0, DEEP), :], send_m.at[0], recv_m.at[0]),
        send_to(-1, 0, win_hbm.at[:, :, head, :], win.at[:, :, pl.ds(DEEP + ROWS, DEEP), :], send_m.at[1], recv_m.at[1]),
    ]
    mixes = [
        send_to(1, 0, mix_out.at[tail], mix_in.at[0], send_m.at[2], recv_m.at[2]),
        send_to(-1, 0, mix_out.at[head], mix_in.at[1], send_m.at[3], recv_m.at[3]),
    ]
    sides = [
        send_to(
            up,
            right,
            side_out.at[0 if right > 0 else 1],
            side_in.at[0 if right > 0 else 1, pl.ds((2 - up) * ROWS, ROWS), :],
            send_s.at[i],
            recv_s.at[i],
        )
        for i, (up, right) in enumerate((up, right) for up in NEAR for right in (-1, 1))
    ]
    end, body = pl.ds(ROWS + DEEP, DEEP), pl.ds(DEEP, ROWS)
    halo = [
        send_to(up, right, source, target, send_a.at[i], recv_a.at[i])
        for i, (up, right, source, target) in enumerate(
            (
                (1, 0, rim_out.at[0], rim_in.at[1]),
                (-1, 0, rim_out.at[1], rim_in.at[0]),
                (0, 1, edge_out.at[0], edge_in.at[1, body]),
                (0, -1, edge_out.at[1], edge_in.at[0, body]),
                (1, 1, edge_out.at[0, tail], edge_in.at[1, head]),
                (1, -1, edge_out.at[1, tail], edge_in.at[0, head]),
                (-1, 1, edge_out.at[0, head], edge_in.at[1, end]),
                (-1, -1, edge_out.at[1, head], edge_in.at[0, end]),
            )
        )
    ]

    pl.semaphore_wait(barrier, len(around))
    for copy in ocean[0] + winds:
        copy.start()

    for load in loads[:4]:
        load.wait()
    pack_ocean(oce, win, side_out)
    for copy in sides:
        copy.start()

    line = lax.broadcasted_iota(jnp.int32, (ROWS, ROWS), 0)
    mark = lax.broadcasted_iota(jnp.int32, (ROWS, ROWS), 1)
    upward = jnp.sum(jnp.where(line == mark, jnp.broadcast_to(off[...], (ROWS, ROWS)), 0), axis=1, keepdims=True) > 0
    upward = jnp.broadcast_to(upward, (ROWS, LANES))
    weights = turn(reg[...].astype(F32), ROWS)
    left = lane_ids(ROWS) < ROWS
    lower = jnp.where(left & upward, 0.0, weights)
    upper = jnp.where(left & upward, weights, 0.0)
    mix_out[:, :LANES] = lower.astype(BF16)
    mix_out[:, LANES:] = upper.astype(BF16)
    for copy in mixes:
        copy.start()
    lower, upper = turn(lower, ROWS), turn(upper, ROWS)
    inner = slice(DEEP, DEEP + ROWS)
    mix[inner, :LANES] = jnp.where(left, 0.0, lower).astype(BF16)
    mix[inner, LANES : 2 * LANES] = jnp.where(left, lower, upper).astype(BF16)
    mix[inner, 2 * LANES :] = jnp.zeros((ROWS, LANES), BF16)

    for load in loads[4:]:
        load.wait()

    lanes_one = lane_ids(1)[:, : cov.shape[1]]
    flags = [
        jnp.sum(jnp.where(lanes_one == 2 * lon + c, cov[...], 0), axis=1, keepdims=True) > 0 for c in range(2)
    ]

    def prepare(i, carry):
        row = pl.multiple_of(i * 8, 8)
        rows = pl.ds(row, 8)
        inside = pl.ds(pl.multiple_of(BASE + row, 8), 8)
        for c in range(2):
            cells = slice(c * LANES, (c + 1) * LANES)
            ext[U][c, inside, :] = vel[0, rows, cells]
            ext[V][c, inside, :] = vel[1, rows, cells]
            one, two = stress[0, rows, cells], stress[1, rows, cells]
            ext[X][c, inside, :] = 0.25 * (one + two)
            ext[Y][c, inside, :] = 0.25 * (one - two)
            ext[S][c, inside, :] = 0.5 * stress[2, rows, cells]
            open_mask = land[rows, cells].astype(F32)
            share = [con[k, rows, cells] for k in range(CATS)]
            thick = [thk[k, rows, cells] for k in range(CATS)]
            area = sum(share[1:], share[0])
            weight = jnp.exp(-2.0 * (1.0 - area)) * open_mask * (1.0 / 12.0)
            volume = sum((share[k] * thick[k] for k in range(1, CATS)), share[0] * thick[0])
            grow = jnp.broadcast_to(flags[c], (8, LANES))
            for bulk, mass in ((B0, E0), (B1, E1)):
                mean = volume / area
                thick = [jnp.where(grow, t + 0.3 / (0.5 + t) + 0.3 * (mean - t), t) for t in thick]
                volume = sum((share[k] * thick[k] for k in range(1, CATS)), share[0] * thick[0])
                ext[bulk][c, inside, :] = volume * weight
                ext[mass][c, inside, :] = 0.5 * open_mask / (volume + 1.0)
            for k in range(CATS):
                thk_out[k, rows, cells] = thick[k]
        return carry

    lax.fori_loop(0, ROWS // 8, prepare, 0)

    pack_sides(ext, rim_out, edge_out)
    for copy in halo + ocean[1]:
        copy.start()

    north_in = jnp.where(lat == lats - 1, 0.0, 1.0).astype(F32)
    south_in = jnp.where(lat == 0, 0.0, 1.0).astype(F32)
    lanes = lane_ids(8)
    first, last = lanes == 0, lanes == LANES - 1
    band = slice(PAD, PAD + WIDE)

    def force(w, mass, fields):
        for part, field in enumerate(fields):
            current = jnp.dot(mix[:, : 5 * ROWS], oce[w, part], preferred_element_type=F32)
            total = current + win[w, part].astype(F32)
            for c in range(2):
                ext[field][c, band, :] = ext[mass][c, band, :] * total[:, c * LANES : (c + 1) * LANES]

    for copy in halo:
        copy.wait_recv()
    unpack_sides(ext, rim_in, edge_in, north_in, south_in)

    reach = DEEP
    for bulk, mass, gx, gy in ((B0, E0, GX0, GY0), (B1, E1, GX1, GY1)):
        for step in range(SUB):
            low, high = tiles_within(reach - 1)
            sweep(low, high, lambda rows: stress_rows(ext, rows, bulk, mass, first, last))
            if step == 0 and bulk == B0:
                for copy in mixes:
                    copy.wait_recv()
                mix[:DEEP, : 2 * LANES] = mix_in[0]
                mix[:DEEP, 2 * LANES :] = jnp.zeros((DEEP, LANES), BF16)
                mix[DEEP + ROWS :, :LANES] = jnp.zeros((DEEP, LANES), BF16)
                mix[DEEP + ROWS :, LANES:] = mix_in[1]
                for copy in sides:
                    copy.wait_recv()
                near = slice(2 * ROWS - DEEP, 3 * ROWS + DEEP)
                flows = [
                    jnp.dot(mix[:, : 5 * ROWS], side_in[d], preferred_element_type=F32)
                    + turn(side_in[d, near, :].astype(F32), ROWS)
                    for d in range(2)
                ]
                is_east = lane_ids(WIDE) < LANES // 2
                for k, (field, weight) in enumerate(((GX0, E0), (GY0, E0), (GX1, E1), (GY1, E1))):
                    total = jnp.where(is_east, turn(flows[1], -DEEP * k), turn(flows[0], LANES - DEEP - DEEP * k))
                    ext[field][2, band, :] = ext[weight][2, band, :] * total
                for copy in winds + ocean[0]:
                    copy.wait_recv()
                force(0, E0, (GX0, GY0))
            if step == 0 and bulk == B1:
                for copy in ocean[1]:
                    copy.wait_recv()
                force(1, E1, (GX1, GY1))
            low, high = tiles_within(reach - 2)
            sweep(low, high, lambda rows: velocity_rows(ext, rows, mass, gx, gy, first, last))
            reach -= 2

    inner = slice(BASE, BASE + ROWS)
    for c in range(2):
        cells = slice(c * LANES, (c + 1) * LANES)
        one, two = ext[X][c, inner, :], ext[Y][c, inner, :]
        str_out[0, :, cells] = 2.0 * (one + two)
        str_out[1, :, cells] = 2.0 * (one - two)
        str_out[2, :, cells] = 2.0 * ext[S][c, inner, :]
        vel_out[0, :, cells] = ext[U][c, inner, :]
        vel_out[1, :, cells] = ext[V][c, inner, :]

    for copy in ocean[0] + ocean[1] + winds + mixes + sides + halo:
        copy.wait_send()


def local(velocity, stress, thickness, concentration, land_mask, covered, ocean_current, wind_stress, regrid_weights, tile_offset):
    offsets = tile_offset.reshape(1, -1)
    arrays = (velocity, stress, thickness, concentration, land_mask, covered, ocean_current, wind_stress, regrid_weights, offsets)
    width = velocity.shape[-1]
    held = {6: (2, 2, 5 * ROWS, width), 7: (2, 2, WIDE, width)}
    staged = [pltpu.VMEM(held.get(i, a.shape), a.dtype) for i, a in enumerate(arrays)]
    field = pltpu.VMEM((3, TALL, LANES), F32)
    rim = pltpu.VMEM((2, len(STATE), 2, DEEP, LANES), BF16)
    dma = pltpu.SemaphoreType.DMA
    return pl.pallas_call(
        kernel,
        out_shape=[pltpu.VMEM(a.shape, F32) for a in (velocity, stress, thickness)],
        in_specs=[pl.BlockSpec(memory_space=pl.ANY)] * len(arrays),
        out_specs=[pl.BlockSpec(memory_space=pltpu.VMEM)] * 3,
        scratch_shapes=staged
        + [field] * 13
        + [
            rim,
            pltpu.VMEM((2, ROWS, LANES), BF16),
            rim,
            pltpu.VMEM((2, WIDE, LANES), BF16),
            pltpu.VMEM((2, ROWS, LANES), BF16),
            pltpu.VMEM((2, 5 * ROWS, LANES), BF16),
            pltpu.VMEM((ROWS, 2 * LANES), BF16),
            pltpu.VMEM((2, DEEP, 2 * LANES), BF16),
            pltpu.VMEM((WIDE, 3 * LANES), BF16),
        ]
        + [dma((n,)) for n in (10, 8, 8, 8, 8, 10, 10, 4, 4)],
        compiler_params=pltpu.CompilerParams(collective_id=0, has_side_effects=True),
    )(*arrays)


def solution(mesh):
    return jax.shard_map(
        local,
        mesh=mesh,
        in_specs=(
            P(None, "lat", "lon"),
            P(None, "lat", "lon"),
            P(None, "lat", "lon"),
            P(None, "lat", "lon"),
            P("lat", "lon"),
            P("lat", None),
            P(None, None, "lat", "lon"),
            P(None, None, "lat", "lon"),
            P("lat", None),
            P("lat"),
        ),
        out_specs=(P(None, "lat", "lon"), P(None, "lat", "lon"), P(None, "lat", "lon")),
        check_vma=False,
    )
```

```python
import jax
import jax.numpy as jnp
from jax import lax
from jax.experimental import pallas as pl
from jax.experimental.pallas import tpu as pltpu
from jax.sharding import PartitionSpec as P

MESH = pl.DeviceIdType.MESH
F32 = jnp.float32
BF16 = jnp.bfloat16

ROWS = 64
LANES = 128
DEEP = 16
PAD = 8
BASE = PAD + DEEP
TALL = ROWS + 2 * BASE
SUB = 4
CATS = 6

U, V, X, Y, S, B0, E0, B1, E1, GX0, GY0, GX1, GY1 = range(13)
STATE = ((U,), (V,), (X,), (Y,), (S,), (B0,), (E0,), (B1, E1))
WIDE = ROWS + 2 * DEEP
NEAR = (-2, -1, 0, 1, 2)
GROUP = 2


def lane_ids(rows):
    return lax.broadcasted_iota(jnp.int32, (rows, LANES), 1)


def turn(value, shift):
    shift = shift % LANES
    return pltpu.roll(value, shift, 1) if shift else value


def pack_sides(ext, rim, edge):
    top, low = BASE + ROWS - DEEP, BASE
    half = DEEP // 2
    for k, block in enumerate(STATE):
        for c in range(2):
            if len(block) == 1:
                rim[0, k, c] = ext[block[0]][c, top : top + DEEP, :].astype(BF16)
                rim[1, k, c] = ext[block[0]][c, low : low + DEEP, :].astype(BF16)
            else:
                one, two = ext[block[0]], ext[block[1]]
                rim[0, k, c] = jnp.concatenate([one[c, top + half : top + DEEP, :], two[c, top + half : top + DEEP, :]], axis=0).astype(BF16)
                rim[1, k, c] = jnp.concatenate([one[c, low : low + half, :], two[c, low : low + half, :]], axis=0).astype(BF16)
    lanes = lane_ids(DEEP)
    for piece in range(ROWS // DEEP):
        rows = slice(BASE + piece * DEEP, BASE + (piece + 1) * DEEP)
        east = jnp.zeros((DEEP, LANES), F32)
        west = jnp.zeros((DEEP, LANES), F32)
        for k, block in enumerate(STATE):
            width = DEEP // len(block)
            for part, field in enumerate(block):
                start = DEEP * k + width * part
                here = (lanes >= start) & (lanes < start + width)
                east = jnp.where(here, turn(ext[field][1, rows, :], start - (LANES - width)), east)
                west = jnp.where(here, turn(ext[field][0, rows, :], start), west)
        edge[0, piece * DEEP : (piece + 1) * DEEP, :] = east.astype(BF16)
        edge[1, piece * DEEP : (piece + 1) * DEEP, :] = west.astype(BF16)


def unpack_sides(ext, rim, edge):
    half = DEEP // 2
    top, low = BASE + ROWS, BASE - DEEP
    for k, block in enumerate(STATE):
        for c in range(2):
            from_north = rim[0, k, c].astype(F32)
            from_south = rim[1, k, c].astype(F32)
            if len(block) == 1:
                ext[block[0]][c, top : top + DEEP, :] = from_north
                ext[block[0]][c, low : low + DEEP, :] = from_south
            else:
                for part, field in enumerate(block):
                    ext[field][c, top : top + half, :] = from_north[part * half : (part + 1) * half]
                    ext[field][c, low + half : low + DEEP, :] = from_south[part * half : (part + 1) * half]
    left = lane_ids(DEEP) < LANES // 2
    pieces = WIDE // DEEP
    for piece in range(pieces):
        rows = slice(piece * DEEP, (piece + 1) * DEEP)
        east = edge[0, rows, :].astype(F32)
        west = edge[1, rows, :].astype(F32)
        for k, block in enumerate(STATE):
            width = DEEP // len(block)
            for part, field in enumerate(block):
                start = DEEP * k + width * part
                ext[field][2, PAD + piece * DEEP : PAD + (piece + 1) * DEEP, :] = jnp.where(
                    left, turn(east, -start), turn(west, LANES - width - start)
                )


def pack_ocean(ocean, wind, side):
    lanes = lane_ids(ROWS)
    east = jnp.zeros((ROWS, LANES), F32)
    west = jnp.zeros((ROWS, LANES), F32)
    for k in range(8):
        w, part = (k % 4) // 2, k % 2
        if k < 4:
            field = ocean[w, part, 2 * ROWS : 3 * ROWS, :]
        else:
            field = wind[w, part, DEEP : DEEP + ROWS, :]
        start = DEEP * k
        here = (lanes >= start) & (lanes < start + DEEP)
        east = jnp.where(here, turn(field[:, LANES:].astype(F32), start + DEEP), east)
        west = jnp.where(here, turn(field[:, :LANES].astype(F32), start), west)
    side[0] = east.astype(BF16)
    side[1] = west.astype(BF16)


def spread(tiles, first, last):
    ahead = [turn(t, -1) for t in tiles]
    behind = [turn(t, 1) for t in tiles]
    return [
        jnp.where(last, ahead[(c + 1) % 3], ahead[c]) - jnp.where(first, behind[(c + 2) % 3], behind[c])
        for c in range(3)
    ]


def stress_rows(ext, rows_list, bulk, mass, first, last):
    results = []
    for row in rows_list:

        def at(field, shift):
            return [ext[field][c, pl.ds(row + shift, 8), :] for c in range(3)]

        du = spread(at(U, 0), first, last)
        dv = spread(at(V, 0), first, last)
        un, us, vn, vs = at(U, 1), at(U, -1), at(V, 1), at(V, -1)
        bs, es, xs, ys, ss = at(bulk, 0), at(mass, 0), at(X, 0), at(Y, 0), at(S, 0)
        for c in range(3):
            up = vn[c] - vs[c]
            shear = (un[c] - us[c]) + dv[c]
            div = du[c] + up
            ten = du[c] - up
            rate = lax.rsqrt(div * div + 0.25 * (ten * ten + shear * shear) + 1.0)
            keep = jnp.where(es[c] > 0.0, 2.0 / 3.0, 0.0)
            br = bs[c] * rate
            quarter = 0.25 * br
            press = br * div - bs[c]
            pull = quarter * ten
            common = keep * xs[c] + press
            other = keep * ys[c] + press
            results.append((row, c, common + pull, other - pull, keep * ss[c] + quarter * shear))
    for row, c, x, y, s in results:
        rows = pl.ds(row, 8)
        ext[X][c, rows, :] = x
        ext[Y][c, rows, :] = y
        ext[S][c, rows, :] = s


def velocity_rows(ext, rows_list, mass, gx, gy, first, last):
    results = []
    for row in rows_list:

        def at(field, shift):
            return [ext[field][c, pl.ds(row + shift, 8), :] for c in range(3)]

        dx = spread(at(X, 0), first, last)
        ds = spread(at(S, 0), first, last)
        yn, ys, sn, ss = at(Y, 1), at(Y, -1), at(S, 1), at(S, -1)
        es, us, vs, gxs, gys = at(mass, 0), at(U, 0), at(V, 0), at(gx, 0), at(gy, 0)
        for c in range(3):
            e = es[c]
            keep = jnp.where(e > 0.0, 1.0 - e, 0.0)
            fx = dx[c] + (sn[c] - ss[c])
            fy = ds[c] + (yn[c] - ys[c])
            results.append((row, c, keep * us[c] + (gxs[c] + e * fx), keep * vs[c] + (gys[c] + e * fy)))
    for row, c, u, v in results:
        rows = pl.ds(row, 8)
        ext[U][c, rows, :] = u
        ext[V][c, rows, :] = v


def tiles_within(reach):
    above = (reach + 7) // 8
    return BASE // 8 - above, BASE // 8 + ROWS // 8 + above


def sweep(low, high, body):
    for start in range(low, high, GROUP):
        body([8 * tile for tile in range(start, min(start + GROUP, high))])


def kernel(
    vel_hbm,
    str_hbm,
    thk_hbm,
    con_hbm,
    land_hbm,
    cov_hbm,
    oce_hbm,
    win_hbm,
    reg_hbm,
    off_hbm,
    vel_out,
    str_out,
    thk_out,
    vel,
    stress,
    thk,
    con,
    land,
    cov,
    oce,
    win,
    reg,
    off,
    u_ref,
    v_ref,
    x_ref,
    y_ref,
    s_ref,
    b0_ref,
    e0_ref,
    b1_ref,
    e1_ref,
    gx0_ref,
    gy0_ref,
    gx1_ref,
    gy1_ref,
    rim_out,
    edge_out,
    rim_in,
    edge_in,
    side_out,
    side_in,
    mix_out,
    mix_in,
    mix,
    load_sem,
    send_a,
    recv_a,
    send_o,
    recv_o,
    send_s,
    recv_s,
    send_m,
    recv_m,
):
    ext = (u_ref, v_ref, x_ref, y_ref, s_ref, b0_ref, e0_ref, b1_ref, e1_ref, gx0_ref, gy0_ref, gx1_ref, gy1_ref)
    lat, lon = lax.axis_index("lat"), lax.axis_index("lon")
    lats, lons = lax.axis_size("lat"), lax.axis_size("lon")

    def place(up, right):
        return lax.rem(lat + lats + up, lats), lax.rem(lon + lons + right, lons)

    def send_to(up, right, source, target, send, recv):
        to_lat, to_lon = place(up, right)
        return up, pltpu.make_async_remote_copy(
            src_ref=source,
            dst_ref=target,
            send_sem=send,
            recv_sem=recv,
            device_id={"lat": to_lat, "lon": to_lon},
            device_id_type=MESH,
        )

    def begin(copies):
        for up, copy in copies:
            only_if(up, copy.start)

    def arrive(copies):
        for up, copy in copies:
            only_if(-up, copy.wait_recv)

    def leave(copies):
        for up, copy in copies:
            only_if(up, copy.wait_send)

    def exists(up):
        return lat + up < lats if up > 0 else lat + up >= 0

    def only_if(up, act):
        if up:
            pl.when(exists(up))(act)
        else:
            act()

    barrier = pltpu.get_barrier_semaphore()
    greeted = jnp.int32(2)
    for up in NEAR:

        def greet(up=up):
            for right in (-1, 0, 1):
                if up or right:
                    to_lat, to_lon = place(up, right)
                    pl.semaphore_signal(barrier, inc=1, device_id={"lat": to_lat, "lon": to_lon}, device_id_type=MESH)

        only_if(up, greet)
        if up:
            greeted = greeted + jnp.where(exists(up), 3, 0)

    own = pl.ds(2 * ROWS, ROWS)
    loads = [
        pltpu.make_async_copy(source, target, load_sem.at[i])
        for i, (source, target) in enumerate(
            (
                (oce_hbm, oce.at[:, :, own, :]),
                (win_hbm, win.at[:, :, pl.ds(DEEP, ROWS), :]),
                (reg_hbm, reg),
                (off_hbm, off),
                (thk_hbm, thk),
                (con_hbm, con),
                (land_hbm, land),
                (cov_hbm, cov),
                (vel_hbm, vel),
                (str_hbm, stress),
            )
        )
    ]
    for load in loads:
        load.start()

    tail, head = pl.ds(ROWS - DEEP, DEEP), pl.ds(0, DEEP)
    ocean = [
        [
            send_to(
                up,
                0,
                oce_hbm.at[w],
                oce.at[w, :, pl.ds((2 - up) * ROWS, ROWS), :],
                send_o.at[4 * w + i],
                recv_o.at[4 * w + i],
            )
            for i, up in enumerate((1, -1, 2, -2))
        ]
        for w in range(2)
    ]
    winds = [
        send_to(1, 0, win_hbm.at[:, :, tail, :], win.at[:, :, pl.ds(0, DEEP), :], send_m.at[0], recv_m.at[0]),
        send_to(-1, 0, win_hbm.at[:, :, head, :], win.at[:, :, pl.ds(DEEP + ROWS, DEEP), :], send_m.at[1], recv_m.at[1]),
    ]
    mixes = [
        send_to(1, 0, mix_out.at[tail], mix_in.at[0], send_m.at[2], recv_m.at[2]),
        send_to(-1, 0, mix_out.at[head], mix_in.at[1], send_m.at[3], recv_m.at[3]),
    ]
    sides = [
        send_to(
            up,
            right,
            side_out.at[0 if right > 0 else 1],
            side_in.at[0 if right > 0 else 1, pl.ds((2 - up) * ROWS, ROWS), :],
            send_s.at[i],
            recv_s.at[i],
        )
        for i, (up, right) in enumerate((up, right) for up in NEAR for right in (-1, 1))
    ]
    end, body = pl.ds(ROWS + DEEP, DEEP), pl.ds(DEEP, ROWS)
    halo = [
        send_to(up, right, source, target, send_a.at[i], recv_a.at[i])
        for i, (up, right, source, target) in enumerate(
            (
                (1, 0, rim_out.at[0], rim_in.at[1]),
                (-1, 0, rim_out.at[1], rim_in.at[0]),
                (0, 1, edge_out.at[0], edge_in.at[1, body]),
                (0, -1, edge_out.at[1], edge_in.at[0, body]),
                (1, 1, edge_out.at[0, tail], edge_in.at[1, head]),
                (1, -1, edge_out.at[1, tail], edge_in.at[0, head]),
                (-1, 1, edge_out.at[0, head], edge_in.at[1, end]),
                (-1, -1, edge_out.at[1, head], edge_in.at[0, end]),
            )
        )
    ]

    pl.semaphore_wait(barrier, greeted)
    begin(ocean[0] + winds)

    def blank(up, parts):
        @pl.when(jnp.logical_not(exists(up)))
        def _():
            for part in parts:
                part[...] = jnp.zeros(part.shape, part.dtype)

    for up, outer, inner_block in ((-1, pl.ds(0, DEEP), 1), (1, pl.ds(DEEP + ROWS, DEEP), 3)):
        beside = pl.ds(inner_block * ROWS, ROWS)
        side = 1 if up < 0 else 0
        blank(up, (rim_in.at[side], edge_in.at[:, outer, :], win.at[:, :, outer, :], mix_in.at[1 - side], oce.at[:, :, beside, :], side_in.at[:, beside, :]))
    for up, block in ((-2, 0), (2, 4)):
        beyond = pl.ds(block * ROWS, ROWS)
        blank(up, (oce.at[:, :, beyond, :], side_in.at[:, beyond, :]))

    for load in loads[:4]:
        load.wait()
    pack_ocean(oce, win, side_out)
    begin(sides)

    line = lax.broadcasted_iota(jnp.int32, (ROWS, ROWS), 0)
    mark = lax.broadcasted_iota(jnp.int32, (ROWS, ROWS), 1)
    upward = jnp.sum(jnp.where(line == mark, jnp.broadcast_to(off[...], (ROWS, ROWS)), 0), axis=1, keepdims=True) > 0
    upward = jnp.broadcast_to(upward, (ROWS, LANES))
    weights = turn(reg[...].astype(F32), ROWS)
    left = lane_ids(ROWS) < ROWS
    lower = jnp.where(left & upward, 0.0, weights)
    upper = jnp.where(left & upward, weights, 0.0)
    mix_out[:, :LANES] = lower.astype(BF16)
    mix_out[:, LANES:] = upper.astype(BF16)
    begin(mixes)
    lower, upper = turn(lower, ROWS), turn(upper, ROWS)
    inner = slice(DEEP, DEEP + ROWS)
    mix[inner, :LANES] = jnp.where(left, 0.0, lower).astype(BF16)
    mix[inner, LANES : 2 * LANES] = jnp.where(left, lower, upper).astype(BF16)
    mix[inner, 2 * LANES :] = jnp.zeros((ROWS, LANES), BF16)

    for load in loads[4:]:
        load.wait()

    lanes_one = lane_ids(1)[:, : cov.shape[1]]
    flags = [
        jnp.sum(jnp.where(lanes_one == 2 * lon + c, cov[...], 0), axis=1, keepdims=True) > 0 for c in range(2)
    ]

    def prepare(i, carry):
        row = pl.multiple_of(i * 8, 8)
        rows = pl.ds(row, 8)
        inside = pl.ds(pl.multiple_of(BASE + row, 8), 8)
        for c in range(2):
            cells = slice(c * LANES, (c + 1) * LANES)
            ext[U][c, inside, :] = vel[0, rows, cells]
            ext[V][c, inside, :] = vel[1, rows, cells]
            one, two = stress[0, rows, cells], stress[1, rows, cells]
            ext[X][c, inside, :] = 0.25 * (one + two)
            ext[Y][c, inside, :] = 0.25 * (one - two)
            ext[S][c, inside, :] = 0.5 * stress[2, rows, cells]
            open_mask = land[rows, cells].astype(F32)
            share = [con[k, rows, cells] for k in range(CATS)]
            thick = [thk[k, rows, cells] for k in range(CATS)]
            area = sum(share[1:], share[0])
            weight = jnp.exp(-2.0 * (1.0 - area)) * open_mask * (1.0 / 12.0)
            volume = sum((share[k] * thick[k] for k in range(1, CATS)), share[0] * thick[0])
            grow = jnp.broadcast_to(flags[c], (8, LANES))
            for bulk, mass in ((B0, E0), (B1, E1)):
                mean = volume / area
                thick = [jnp.where(grow, t + 0.3 / (0.5 + t) + 0.3 * (mean - t), t) for t in thick]
                volume = sum((share[k] * thick[k] for k in range(1, CATS)), share[0] * thick[0])
                ext[bulk][c, inside, :] = volume * weight
                ext[mass][c, inside, :] = 0.5 * open_mask / (volume + 1.0)
            for k in range(CATS):
                thk_out[k, rows, cells] = thick[k]
        return carry

    lax.fori_loop(0, ROWS // 8, prepare, 0)

    pack_sides(ext, rim_out, edge_out)
    begin(halo + ocean[1])

    lanes = lane_ids(8)
    first, last = lanes == 0, lanes == LANES - 1
    band = slice(PAD, PAD + WIDE)

    def force(w, mass, fields):
        for part, field in enumerate(fields):
            current = jnp.dot(mix[:, : 5 * ROWS], oce[w, part], preferred_element_type=F32)
            total = current + win[w, part].astype(F32)
            for c in range(2):
                ext[field][c, band, :] = ext[mass][c, band, :] * total[:, c * LANES : (c + 1) * LANES]

    arrive(halo)
    unpack_sides(ext, rim_in, edge_in)

    reach = DEEP
    for bulk, mass, gx, gy in ((B0, E0, GX0, GY0), (B1, E1, GX1, GY1)):
        for step in range(SUB):
            low, high = tiles_within(reach - 1)
            sweep(low, high, lambda rows: stress_rows(ext, rows, bulk, mass, first, last))
            if step == 0 and bulk == B0:
                arrive(mixes)
                mix[:DEEP, : 2 * LANES] = mix_in[0]
                mix[:DEEP, 2 * LANES :] = jnp.zeros((DEEP, LANES), BF16)
                mix[DEEP + ROWS :, :LANES] = jnp.zeros((DEEP, LANES), BF16)
                mix[DEEP + ROWS :, LANES:] = mix_in[1]
                arrive(sides)
                near = slice(2 * ROWS - DEEP, 3 * ROWS + DEEP)
                flows = [
                    jnp.dot(mix[:, : 5 * ROWS], side_in[d], preferred_element_type=F32)
                    + turn(side_in[d, near, :].astype(F32), ROWS)
                    for d in range(2)
                ]
                is_east = lane_ids(WIDE) < LANES // 2
                for k, (field, weight) in enumerate(((GX0, E0), (GY0, E0), (GX1, E1), (GY1, E1))):
                    total = jnp.where(is_east, turn(flows[1], -DEEP * k), turn(flows[0], LANES - DEEP - DEEP * k))
                    ext[field][2, band, :] = ext[weight][2, band, :] * total
                arrive(winds + ocean[0])
                force(0, E0, (GX0, GY0))
            if step == 0 and bulk == B1:
                arrive(ocean[1])
                force(1, E1, (GX1, GY1))
            low, high = tiles_within(reach - 2)
            sweep(low, high, lambda rows: velocity_rows(ext, rows, mass, gx, gy, first, last))
            reach -= 2

    inner = slice(BASE, BASE + ROWS)
    for c in range(2):
        cells = slice(c * LANES, (c + 1) * LANES)
        one, two = ext[X][c, inner, :], ext[Y][c, inner, :]
        str_out[0, :, cells] = 2.0 * (one + two)
        str_out[1, :, cells] = 2.0 * (one - two)
        str_out[2, :, cells] = 2.0 * ext[S][c, inner, :]
        vel_out[0, :, cells] = ext[U][c, inner, :]
        vel_out[1, :, cells] = ext[V][c, inner, :]

    leave(ocean[0] + ocean[1] + winds + mixes + sides + halo)


def local(velocity, stress, thickness, concentration, land_mask, covered, ocean_current, wind_stress, regrid_weights, tile_offset):
    offsets = tile_offset.reshape(1, -1)
    arrays = (velocity, stress, thickness, concentration, land_mask, covered, ocean_current, wind_stress, regrid_weights, offsets)
    width = velocity.shape[-1]
    held = {6: (2, 2, 5 * ROWS, width), 7: (2, 2, WIDE, width)}
    staged = [pltpu.VMEM(held.get(i, a.shape), a.dtype) for i, a in enumerate(arrays)]
    field = pltpu.VMEM((3, TALL, LANES), F32)
    rim = pltpu.VMEM((2, len(STATE), 2, DEEP, LANES), BF16)
    dma = pltpu.SemaphoreType.DMA
    return pl.pallas_call(
        kernel,
        out_shape=[pltpu.VMEM(a.shape, F32) for a in (velocity, stress, thickness)],
        in_specs=[pl.BlockSpec(memory_space=pl.ANY)] * len(arrays),
        out_specs=[pl.BlockSpec(memory_space=pltpu.VMEM)] * 3,
        scratch_shapes=staged
        + [field] * 13
        + [
            rim,
            pltpu.VMEM((2, ROWS, LANES), BF16),
            rim,
            pltpu.VMEM((2, WIDE, LANES), BF16),
            pltpu.VMEM((2, ROWS, LANES), BF16),
            pltpu.VMEM((2, 5 * ROWS, LANES), BF16),
            pltpu.VMEM((ROWS, 2 * LANES), BF16),
            pltpu.VMEM((2, DEEP, 2 * LANES), BF16),
            pltpu.VMEM((WIDE, 3 * LANES), BF16),
        ]
        + [dma((n,)) for n in (10, 8, 8, 8, 8, 10, 10, 4, 4)],
        compiler_params=pltpu.CompilerParams(collective_id=0, has_side_effects=True),
    )(*arrays)


def solution(mesh):
    return jax.shard_map(
        local,
        mesh=mesh,
        in_specs=(
            P(None, "lat", "lon"),
            P(None, "lat", "lon"),
            P(None, "lat", "lon"),
            P(None, "lat", "lon"),
            P("lat", "lon"),
            P("lat", None),
            P(None, None, "lat", "lon"),
            P(None, None, "lat", "lon"),
            P("lat", None),
            P("lat"),
        ),
        out_specs=(P(None, "lat", "lon"), P(None, "lat", "lon"), P(None, "lat", "lon")),
        check_vma=False,
    )
```

```python
import jax
import jax.numpy as jnp
from jax import lax
from jax.experimental import pallas as pl
from jax.experimental.pallas import tpu as pltpu
from jax.sharding import PartitionSpec as P

MESH = pl.DeviceIdType.MESH
F32 = jnp.float32
BF16 = jnp.bfloat16

ROWS = 64
LANES = 128
DEEP = 16
PAD = 8
BASE = PAD + DEEP
TALL = ROWS + 2 * BASE
SUB = 4
CATS = 6

U, V, X, Y, S, B0, E0, B1, E1, GX0, GY0, GX1, GY1 = range(13)
STATE = ((U,), (V,), (X,), (Y,), (S,), (B0,), (E0,), (B1, E1))
WIDE = ROWS + 2 * DEEP
NEAR = (-2, -1, 0, 1, 2)
GROUP = 2


def lane_ids(rows):
    return lax.broadcasted_iota(jnp.int32, (rows, LANES), 1)


def turn(value, shift):
    shift = shift % LANES
    return pltpu.roll(value, shift, 1) if shift else value


def pack_sides(ext, rim, edge):
    top, low = BASE + ROWS - DEEP, BASE
    half = DEEP // 2
    for k, block in enumerate(STATE):
        for c in range(2):
            if len(block) == 1:
                rim[0, k, c] = ext[block[0]][c, top : top + DEEP, :].astype(BF16)
                rim[1, k, c] = ext[block[0]][c, low : low + DEEP, :].astype(BF16)
            else:
                one, two = ext[block[0]], ext[block[1]]
                rim[0, k, c] = jnp.concatenate([one[c, top + half : top + DEEP, :], two[c, top + half : top + DEEP, :]], axis=0).astype(BF16)
                rim[1, k, c] = jnp.concatenate([one[c, low : low + half, :], two[c, low : low + half, :]], axis=0).astype(BF16)
    lanes = lane_ids(DEEP)
    for piece in range(ROWS // DEEP):
        rows = slice(BASE + piece * DEEP, BASE + (piece + 1) * DEEP)
        east = jnp.zeros((DEEP, LANES), F32)
        west = jnp.zeros((DEEP, LANES), F32)
        for k, block in enumerate(STATE):
            width = DEEP // len(block)
            for part, field in enumerate(block):
                start = DEEP * k + width * part
                here = (lanes >= start) & (lanes < start + width)
                east = jnp.where(here, turn(ext[field][1, rows, :], start - (LANES - width)), east)
                west = jnp.where(here, turn(ext[field][0, rows, :], start), west)
        edge[0, piece * DEEP : (piece + 1) * DEEP, :] = east.astype(BF16)
        edge[1, piece * DEEP : (piece + 1) * DEEP, :] = west.astype(BF16)


def unpack_sides(ext, rim, edge):
    half = DEEP // 2
    top, low = BASE + ROWS, BASE - DEEP
    for k, block in enumerate(STATE):
        for c in range(2):
            from_north = rim[0, k, c].astype(F32)
            from_south = rim[1, k, c].astype(F32)
            if len(block) == 1:
                ext[block[0]][c, top : top + DEEP, :] = from_north
                ext[block[0]][c, low : low + DEEP, :] = from_south
            else:
                for part, field in enumerate(block):
                    ext[field][c, top : top + half, :] = from_north[part * half : (part + 1) * half]
                    ext[field][c, low + half : low + DEEP, :] = from_south[part * half : (part + 1) * half]
    left = lane_ids(DEEP) < LANES // 2
    pieces = WIDE // DEEP
    for piece in range(pieces):
        rows = slice(piece * DEEP, (piece + 1) * DEEP)
        east = edge[0, rows, :].astype(F32)
        west = edge[1, rows, :].astype(F32)
        for k, block in enumerate(STATE):
            width = DEEP // len(block)
            for part, field in enumerate(block):
                start = DEEP * k + width * part
                ext[field][2, PAD + piece * DEEP : PAD + (piece + 1) * DEEP, :] = jnp.where(
                    left, turn(east, -start), turn(west, LANES - width - start)
                )


def pack_ocean(ocean, wind, side):
    lanes = lane_ids(ROWS)
    east = jnp.zeros((ROWS, LANES), F32)
    west = jnp.zeros((ROWS, LANES), F32)
    for k in range(8):
        w, part = (k % 4) // 2, k % 2
        if k < 4:
            field = ocean[w, part, 2 * ROWS : 3 * ROWS, :]
        else:
            field = wind[w, part, DEEP : DEEP + ROWS, :]
        start = DEEP * k
        here = (lanes >= start) & (lanes < start + DEEP)
        east = jnp.where(here, turn(field[:, LANES:].astype(F32), start + DEEP), east)
        west = jnp.where(here, turn(field[:, :LANES].astype(F32), start), west)
    side[0] = east.astype(BF16)
    side[1] = west.astype(BF16)


def spread(tiles, first, last):
    ahead = [turn(t, -1) for t in tiles]
    behind = [turn(t, 1) for t in tiles]
    return [
        jnp.where(last, ahead[(c + 1) % 3], ahead[c]) - jnp.where(first, behind[(c + 2) % 3], behind[c])
        for c in range(3)
    ]


def stress_rows(ext, rows_list, bulk, mass, first, last):
    results = []
    for row in rows_list:

        def at(field, shift):
            return [ext[field][c, pl.ds(row + shift, 8), :] for c in range(3)]

        du = spread(at(U, 0), first, last)
        dv = spread(at(V, 0), first, last)
        un, us, vn, vs = at(U, 1), at(U, -1), at(V, 1), at(V, -1)
        bs, es, xs, ys, ss = at(bulk, 0), at(mass, 0), at(X, 0), at(Y, 0), at(S, 0)
        for c in range(3):
            up = vn[c] - vs[c]
            shear = (un[c] - us[c]) + dv[c]
            div = du[c] + up
            ten = du[c] - up
            rate = lax.rsqrt(div * div + 0.25 * (ten * ten + shear * shear) + 1.0)
            keep = jnp.where(es[c] > 0.0, 2.0 / 3.0, 0.0)
            br = bs[c] * rate
            quarter = 0.25 * br
            press = br * div - bs[c]
            pull = quarter * ten
            common = keep * xs[c] + press
            other = keep * ys[c] + press
            results.append((row, c, common + pull, other - pull, keep * ss[c] + quarter * shear))
    for row, c, x, y, s in results:
        rows = pl.ds(row, 8)
        ext[X][c, rows, :] = x
        ext[Y][c, rows, :] = y
        ext[S][c, rows, :] = s


def velocity_rows(ext, rows_list, mass, gx, gy, first, last):
    results = []
    for row in rows_list:

        def at(field, shift):
            return [ext[field][c, pl.ds(row + shift, 8), :] for c in range(3)]

        dx = spread(at(X, 0), first, last)
        ds = spread(at(S, 0), first, last)
        yn, ys, sn, ss = at(Y, 1), at(Y, -1), at(S, 1), at(S, -1)
        es, us, vs, gxs, gys = at(mass, 0), at(U, 0), at(V, 0), at(gx, 0), at(gy, 0)
        for c in range(3):
            e = es[c]
            keep = jnp.where(e > 0.0, 1.0 - e, 0.0)
            fx = dx[c] + (sn[c] - ss[c])
            fy = ds[c] + (yn[c] - ys[c])
            results.append((row, c, keep * us[c] + (gxs[c] + e * fx), keep * vs[c] + (gys[c] + e * fy)))
    for row, c, u, v in results:
        rows = pl.ds(row, 8)
        ext[U][c, rows, :] = u
        ext[V][c, rows, :] = v


def tiles_within(reach):
    above = (reach + 7) // 8
    return BASE // 8 - above, BASE // 8 + ROWS // 8 + above


def sweep(low, high, body):
    for start in range(low, high, GROUP):
        body([8 * tile for tile in range(start, min(start + GROUP, high))])


def kernel(
    vel_hbm,
    str_hbm,
    thk_hbm,
    con_hbm,
    land_hbm,
    cov_hbm,
    oce_hbm,
    win_hbm,
    reg_hbm,
    off_hbm,
    vel_out,
    str_out,
    thk_out,
    vel,
    stress,
    thk,
    con,
    land,
    cov,
    oce,
    win,
    reg,
    off,
    u_ref,
    v_ref,
    x_ref,
    y_ref,
    s_ref,
    b0_ref,
    e0_ref,
    b1_ref,
    e1_ref,
    gx0_ref,
    gy0_ref,
    gx1_ref,
    gy1_ref,
    rim_out,
    edge_out,
    rim_in,
    edge_in,
    side_out,
    side_in,
    mix_out,
    mix_in,
    mix,
    load_sem,
    send_a,
    recv_a,
    send_o,
    recv_o,
    send_s,
    recv_s,
    send_m,
    recv_m,
):
    ext = (u_ref, v_ref, x_ref, y_ref, s_ref, b0_ref, e0_ref, b1_ref, e1_ref, gx0_ref, gy0_ref, gx1_ref, gy1_ref)
    lat, lon = lax.axis_index("lat"), lax.axis_index("lon")
    lats, lons = lax.axis_size("lat"), lax.axis_size("lon")

    def place(up, right):
        return lax.rem(lat + lats + up, lats), lax.rem(lon + lons + right, lons)

    def send_to(up, right, source, target, send, recv):
        to_lat, to_lon = place(up, right)
        return up, pltpu.make_async_remote_copy(
            src_ref=source,
            dst_ref=target,
            send_sem=send,
            recv_sem=recv,
            device_id={"lat": to_lat, "lon": to_lon},
            device_id_type=MESH,
        )

    def begin(copies):
        for up, copy in copies:
            only_if(up, copy.start)

    def arrive(copies):
        for up, copy in copies:
            only_if(-up, copy.wait_recv)

    def leave(copies):
        for up, copy in copies:
            only_if(up, copy.wait_send)

    def exists(up):
        return lat + up < lats if up > 0 else lat + up >= 0

    def only_if(up, act):
        if up:
            pl.when(exists(up))(act)
        else:
            act()

    barrier = pltpu.get_barrier_semaphore()
    greeted = jnp.int32(2)
    for up in NEAR:

        def greet(up=up):
            for right in (-1, 0, 1):
                if up or right:
                    to_lat, to_lon = place(up, right)
                    pl.semaphore_signal(barrier, inc=1, device_id={"lat": to_lat, "lon": to_lon}, device_id_type=MESH)

        only_if(up, greet)
        if up:
            greeted = greeted + jnp.where(exists(up), 3, 0)

    own = pl.ds(2 * ROWS, ROWS)
    loads = [
        pltpu.make_async_copy(source, target, load_sem.at[i])
        for i, (source, target) in enumerate(
            (
                (oce_hbm, oce.at[:, :, own, :]),
                (win_hbm, win.at[:, :, pl.ds(DEEP, ROWS), :]),
                (reg_hbm, reg),
                (off_hbm, off),
                (thk_hbm, thk),
                (con_hbm, con),
                (land_hbm, land),
                (cov_hbm, cov),
                (vel_hbm, vel),
                (str_hbm, stress),
            )
        )
    ]
    for load in loads:
        load.start()

    tail, head = pl.ds(ROWS - DEEP, DEEP), pl.ds(0, DEEP)
    ocean = [
        [
            send_to(
                up,
                0,
                oce_hbm.at[w],
                oce.at[w, :, pl.ds((2 - up) * ROWS, ROWS), :],
                send_o.at[4 * w + i],
                recv_o.at[4 * w + i],
            )
            for i, up in enumerate((2, -2))
        ]
        for w in range(2)
    ]
    stride = 1 - 2 * lax.rem(lat, 2)
    given = pl.ds(pl.multiple_of((2 - stride) * ROWS, ROWS), ROWS)
    taken = pl.ds(pl.multiple_of((2 + stride) * ROWS, ROWS), ROWS)
    pairs = [
        send_to(stride, 0, oce_hbm.at[w], oce.at[w, :, given, :], send_o.at[4 * w + 2], recv_o.at[4 * w + 2])[1]
        for w in range(2)
    ]
    relays = [
        send_to(2 * stride, 0, oce.at[w, :, taken, :], oce.at[w, :, given, :], send_o.at[4 * w + 3], recv_o.at[4 * w + 3])[1]
        for w in range(2)
    ]
    passes_on = (lat + 2 * stride >= 0) & (lat + 2 * stride < lats)
    is_passed = (lat - 2 * stride >= 0) & (lat - 2 * stride < lats)
    winds = [
        send_to(1, 0, win_hbm.at[:, :, tail, :], win.at[:, :, pl.ds(0, DEEP), :], send_m.at[0], recv_m.at[0]),
        send_to(-1, 0, win_hbm.at[:, :, head, :], win.at[:, :, pl.ds(DEEP + ROWS, DEEP), :], send_m.at[1], recv_m.at[1]),
    ]
    mixes = [
        send_to(1, 0, mix_out.at[tail], mix_in.at[0], send_m.at[2], recv_m.at[2]),
        send_to(-1, 0, mix_out.at[head], mix_in.at[1], send_m.at[3], recv_m.at[3]),
    ]
    sides = [
        send_to(
            up,
            right,
            side_out.at[0 if right > 0 else 1],
            side_in.at[0 if right > 0 else 1, pl.ds((2 - up) * ROWS, ROWS), :],
            send_s.at[i],
            recv_s.at[i],
        )
        for i, (up, right) in enumerate((up, right) for up in NEAR for right in (-1, 1))
    ]
    end, body = pl.ds(ROWS + DEEP, DEEP), pl.ds(DEEP, ROWS)
    halo = [
        send_to(up, right, source, target, send_a.at[i], recv_a.at[i])
        for i, (up, right, source, target) in enumerate(
            (
                (1, 0, rim_out.at[0], rim_in.at[1]),
                (-1, 0, rim_out.at[1], rim_in.at[0]),
                (0, 1, edge_out.at[0], edge_in.at[1, body]),
                (0, -1, edge_out.at[1], edge_in.at[0, body]),
                (1, 1, edge_out.at[0, tail], edge_in.at[1, head]),
                (1, -1, edge_out.at[1, tail], edge_in.at[0, head]),
                (-1, 1, edge_out.at[0, head], edge_in.at[1, end]),
                (-1, -1, edge_out.at[1, head], edge_in.at[0, end]),
            )
        )
    ]

    pl.semaphore_wait(barrier, greeted)
    pairs[0].start()
    begin(ocean[0])
    pairs[1].start()
    begin(ocean[1] + winds)

    def blank(up, parts):
        @pl.when(jnp.logical_not(exists(up)))
        def _():
            for part in parts:
                part[...] = jnp.zeros(part.shape, part.dtype)

    for up, outer, inner_block in ((-1, pl.ds(0, DEEP), 1), (1, pl.ds(DEEP + ROWS, DEEP), 3)):
        beside = pl.ds(inner_block * ROWS, ROWS)
        side = 1 if up < 0 else 0
        blank(up, (rim_in.at[side], edge_in.at[:, outer, :], win.at[:, :, outer, :], mix_in.at[1 - side], oce.at[:, :, beside, :], side_in.at[:, beside, :]))
    for up, block in ((-2, 0), (2, 4)):
        beyond = pl.ds(block * ROWS, ROWS)
        blank(up, (oce.at[:, :, beyond, :], side_in.at[:, beyond, :]))

    for load in loads[:4]:
        load.wait()
    pack_ocean(oce, win, side_out)
    begin(sides)

    line = lax.broadcasted_iota(jnp.int32, (ROWS, ROWS), 0)
    mark = lax.broadcasted_iota(jnp.int32, (ROWS, ROWS), 1)
    upward = jnp.sum(jnp.where(line == mark, jnp.broadcast_to(off[...], (ROWS, ROWS)), 0), axis=1, keepdims=True) > 0
    upward = jnp.broadcast_to(upward, (ROWS, LANES))
    weights = turn(reg[...].astype(F32), ROWS)
    left = lane_ids(ROWS) < ROWS
    lower = jnp.where(left & upward, 0.0, weights)
    upper = jnp.where(left & upward, weights, 0.0)
    mix_out[:, :LANES] = lower.astype(BF16)
    mix_out[:, LANES:] = upper.astype(BF16)
    begin(mixes)
    lower, upper = turn(lower, ROWS), turn(upper, ROWS)
    inner = slice(DEEP, DEEP + ROWS)
    mix[inner, :LANES] = jnp.where(left, 0.0, lower).astype(BF16)
    mix[inner, LANES : 2 * LANES] = jnp.where(left, lower, upper).astype(BF16)
    mix[inner, 2 * LANES :] = jnp.zeros((ROWS, LANES), BF16)

    for load in loads[4:]:
        load.wait()

    lanes_one = lane_ids(1)[:, : cov.shape[1]]
    flags = [
        jnp.sum(jnp.where(lanes_one == 2 * lon + c, cov[...], 0), axis=1, keepdims=True) > 0 for c in range(2)
    ]

    def prepare(i, carry):
        row = pl.multiple_of(i * 8, 8)
        rows = pl.ds(row, 8)
        inside = pl.ds(pl.multiple_of(BASE + row, 8), 8)
        for c in range(2):
            cells = slice(c * LANES, (c + 1) * LANES)
            ext[U][c, inside, :] = vel[0, rows, cells]
            ext[V][c, inside, :] = vel[1, rows, cells]
            one, two = stress[0, rows, cells], stress[1, rows, cells]
            ext[X][c, inside, :] = 0.25 * (one + two)
            ext[Y][c, inside, :] = 0.25 * (one - two)
            ext[S][c, inside, :] = 0.5 * stress[2, rows, cells]
            open_mask = land[rows, cells].astype(F32)
            share = [con[k, rows, cells] for k in range(CATS)]
            thick = [thk[k, rows, cells] for k in range(CATS)]
            area = sum(share[1:], share[0])
            weight = jnp.exp(-2.0 * (1.0 - area)) * open_mask * (1.0 / 12.0)
            volume = sum((share[k] * thick[k] for k in range(1, CATS)), share[0] * thick[0])
            grow = jnp.broadcast_to(flags[c], (8, LANES))
            for bulk, mass in ((B0, E0), (B1, E1)):
                mean = volume / area
                thick = [jnp.where(grow, t + 0.3 / (0.5 + t) + 0.3 * (mean - t), t) for t in thick]
                volume = sum((share[k] * thick[k] for k in range(1, CATS)), share[0] * thick[0])
                ext[bulk][c, inside, :] = volume * weight
                ext[mass][c, inside, :] = 0.5 * open_mask / (volume + 1.0)
            for k in range(CATS):
                thk_out[k, rows, cells] = thick[k]
        return carry

    lax.fori_loop(0, ROWS // 8, prepare, 0)

    pack_sides(ext, rim_out, edge_out)
    begin(halo)
    for pair, relay in zip(pairs, relays):
        pair.wait_recv()
        pl.when(passes_on)(relay.start)

    lanes = lane_ids(8)
    first, last = lanes == 0, lanes == LANES - 1
    band = slice(PAD, PAD + WIDE)

    def force(w, mass, fields):
        for part, field in enumerate(fields):
            current = jnp.dot(mix[:, : 5 * ROWS], oce[w, part], preferred_element_type=F32)
            total = current + win[w, part].astype(F32)
            for c in range(2):
                ext[field][c, band, :] = ext[mass][c, band, :] * total[:, c * LANES : (c + 1) * LANES]

    arrive(halo)
    unpack_sides(ext, rim_in, edge_in)

    reach = DEEP
    for bulk, mass, gx, gy in ((B0, E0, GX0, GY0), (B1, E1, GX1, GY1)):
        for step in range(SUB):
            low, high = tiles_within(reach - 1)
            sweep(low, high, lambda rows: stress_rows(ext, rows, bulk, mass, first, last))
            if step == 0 and bulk == B0:
                arrive(mixes)
                mix[:DEEP, : 2 * LANES] = mix_in[0]
                mix[:DEEP, 2 * LANES :] = jnp.zeros((DEEP, LANES), BF16)
                mix[DEEP + ROWS :, :LANES] = jnp.zeros((DEEP, LANES), BF16)
                mix[DEEP + ROWS :, LANES:] = mix_in[1]
                arrive(sides)
                near = slice(2 * ROWS - DEEP, 3 * ROWS + DEEP)
                flows = [
                    jnp.dot(mix[:, : 5 * ROWS], side_in[d], preferred_element_type=F32)
                    + turn(side_in[d, near, :].astype(F32), ROWS)
                    for d in range(2)
                ]
                is_east = lane_ids(WIDE) < LANES // 2
                for k, (field, weight) in enumerate(((GX0, E0), (GY0, E0), (GX1, E1), (GY1, E1))):
                    total = jnp.where(is_east, turn(flows[1], -DEEP * k), turn(flows[0], LANES - DEEP - DEEP * k))
                    ext[field][2, band, :] = ext[weight][2, band, :] * total
                arrive(winds + ocean[0])
                pl.when(is_passed)(relays[0].wait_recv)
                force(0, E0, (GX0, GY0))
            if step == 0 and bulk == B1:
                arrive(ocean[1])
                pl.when(is_passed)(relays[1].wait_recv)
                force(1, E1, (GX1, GY1))
            low, high = tiles_within(reach - 2)
            sweep(low, high, lambda rows: velocity_rows(ext, rows, mass, gx, gy, first, last))
            reach -= 2

    inner = slice(BASE, BASE + ROWS)
    for c in range(2):
        cells = slice(c * LANES, (c + 1) * LANES)
        one, two = ext[X][c, inner, :], ext[Y][c, inner, :]
        str_out[0, :, cells] = 2.0 * (one + two)
        str_out[1, :, cells] = 2.0 * (one - two)
        str_out[2, :, cells] = 2.0 * ext[S][c, inner, :]
        vel_out[0, :, cells] = ext[U][c, inner, :]
        vel_out[1, :, cells] = ext[V][c, inner, :]

    leave(ocean[0] + ocean[1] + winds + mixes + sides + halo)
    for pair, relay in zip(pairs, relays):
        pair.wait_send()
        pl.when(passes_on)(relay.wait_send)


def deliver(vel, stress, thick, vel_out, str_out, thk_out, sems):
    copies = [
        pltpu.make_async_copy(source, target, sems.at[i])
        for i, (source, target) in enumerate(((vel, vel_out), (stress, str_out), (thick, thk_out)))
    ]
    for copy in copies:
        copy.start()
    for copy in copies:
        copy.wait()


def local(velocity, stress, thickness, concentration, land_mask, covered, ocean_current, wind_stress, regrid_weights, tile_offset):
    offsets = tile_offset.reshape(1, -1)
    arrays = (velocity, stress, thickness, concentration, land_mask, covered, ocean_current, wind_stress, regrid_weights, offsets)
    width = velocity.shape[-1]
    held = {6: (2, 2, 5 * ROWS, width), 7: (2, 2, WIDE, width)}
    staged = [pltpu.VMEM(held.get(i, a.shape), a.dtype) for i, a in enumerate(arrays)]
    field = pltpu.VMEM((3, TALL, LANES), F32)
    rim = pltpu.VMEM((2, len(STATE), 2, DEEP, LANES), BF16)
    dma = pltpu.SemaphoreType.DMA
    results = pl.pallas_call(
        kernel,
        out_shape=[pltpu.VMEM(a.shape, F32) for a in (velocity, stress, thickness)],
        in_specs=[pl.BlockSpec(memory_space=pl.ANY)] * len(arrays),
        out_specs=[pl.BlockSpec(memory_space=pltpu.VMEM)] * 3,
        scratch_shapes=staged
        + [field] * 13
        + [
            rim,
            pltpu.VMEM((2, ROWS, LANES), BF16),
            rim,
            pltpu.VMEM((2, WIDE, LANES), BF16),
            pltpu.VMEM((2, ROWS, LANES), BF16),
            pltpu.VMEM((2, 5 * ROWS, LANES), BF16),
            pltpu.VMEM((ROWS, 2 * LANES), BF16),
            pltpu.VMEM((2, DEEP, 2 * LANES), BF16),
            pltpu.VMEM((WIDE, 3 * LANES), BF16),
        ]
        + [dma((n,)) for n in (10, 8, 8, 8, 8, 10, 10, 4, 4)],
        compiler_params=pltpu.CompilerParams(collective_id=0, has_side_effects=True),
    )(*arrays)

    return pl.pallas_call(
        deliver,
        out_shape=[jax.ShapeDtypeStruct(a.shape, F32) for a in (velocity, stress, thickness)],
        in_specs=[pl.BlockSpec(memory_space=pltpu.VMEM)] * 3,
        out_specs=[pl.BlockSpec(memory_space=pl.ANY)] * 3,
        scratch_shapes=[dma((3,))],
    )(*[pltpu.with_memory_space_constraint(r, pltpu.VMEM) for r in results])


def solution(mesh):
    return jax.shard_map(
        local,
        mesh=mesh,
        in_specs=(
            P(None, "lat", "lon"),
            P(None, "lat", "lon"),
            P(None, "lat", "lon"),
            P(None, "lat", "lon"),
            P("lat", "lon"),
            P("lat", None),
            P(None, None, "lat", "lon"),
            P(None, None, "lat", "lon"),
            P("lat", None),
            P("lat"),
        ),
        out_specs=(P(None, "lat", "lon"), P(None, "lat", "lon"), P(None, "lat", "lon")),
        check_vma=False,
    )
```

```python
import jax
import jax.numpy as jnp
from jax import lax
from jax.experimental import pallas as pl
from jax.experimental.pallas import tpu as pltpu
from jax.sharding import PartitionSpec as P

MESH = pl.DeviceIdType.MESH
F32 = jnp.float32
BF16 = jnp.bfloat16

ROWS = 64
LANES = 128
DEEP = 16
PAD = 8
BASE = PAD + DEEP
TALL = ROWS + 2 * BASE
SUB = 4
CATS = 6

U, V, X, Y, S, B0, E0, B1, E1, GX0, GY0, GX1, GY1 = range(13)
STATE = ((U,), (V,), (X,), (Y,), (S,), (B0,), (E0,), (B1, E1))
WIDE = ROWS + 2 * DEEP
NEAR = (-2, -1, 0, 1, 2)
GROUP = 2


def lane_ids(rows):
    return lax.broadcasted_iota(jnp.int32, (rows, LANES), 1)


def turn(value, shift):
    shift = shift % LANES
    return pltpu.roll(value, shift, 1) if shift else value


def pack_sides(ext, rim, edge):
    top, low = BASE + ROWS - DEEP, BASE
    half = DEEP // 2
    for k, block in enumerate(STATE):
        for c in range(2):
            if len(block) == 1:
                rim[0, k, c] = ext[block[0]][c, top : top + DEEP, :].astype(BF16)
                rim[1, k, c] = ext[block[0]][c, low : low + DEEP, :].astype(BF16)
            else:
                one, two = ext[block[0]], ext[block[1]]
                rim[0, k, c] = jnp.concatenate([one[c, top + half : top + DEEP, :], two[c, top + half : top + DEEP, :]], axis=0).astype(BF16)
                rim[1, k, c] = jnp.concatenate([one[c, low : low + half, :], two[c, low : low + half, :]], axis=0).astype(BF16)
    lanes = lane_ids(DEEP)
    for piece in range(ROWS // DEEP):
        rows = slice(BASE + piece * DEEP, BASE + (piece + 1) * DEEP)
        east = jnp.zeros((DEEP, LANES), F32)
        west = jnp.zeros((DEEP, LANES), F32)
        for k, block in enumerate(STATE):
            width = DEEP // len(block)
            for part, field in enumerate(block):
                start = DEEP * k + width * part
                here = (lanes >= start) & (lanes < start + width)
                east = jnp.where(here, turn(ext[field][1, rows, :], start - (LANES - width)), east)
                west = jnp.where(here, turn(ext[field][0, rows, :], start), west)
        edge[0, piece * DEEP : (piece + 1) * DEEP, :] = east.astype(BF16)
        edge[1, piece * DEEP : (piece + 1) * DEEP, :] = west.astype(BF16)


def unpack_sides(ext, rim, edge):
    half = DEEP // 2
    top, low = BASE + ROWS, BASE - DEEP
    for k, block in enumerate(STATE):
        for c in range(2):
            from_north = rim[0, k, c].astype(F32)
            from_south = rim[1, k, c].astype(F32)
            if len(block) == 1:
                ext[block[0]][c, top : top + DEEP, :] = from_north
                ext[block[0]][c, low : low + DEEP, :] = from_south
            else:
                for part, field in enumerate(block):
                    ext[field][c, top : top + half, :] = from_north[part * half : (part + 1) * half]
                    ext[field][c, low + half : low + DEEP, :] = from_south[part * half : (part + 1) * half]
    left = lane_ids(DEEP) < LANES // 2
    pieces = WIDE // DEEP
    for piece in range(pieces):
        rows = slice(piece * DEEP, (piece + 1) * DEEP)
        east = edge[0, rows, :].astype(F32)
        west = edge[1, rows, :].astype(F32)
        for k, block in enumerate(STATE):
            width = DEEP // len(block)
            for part, field in enumerate(block):
                start = DEEP * k + width * part
                ext[field][2, PAD + piece * DEEP : PAD + (piece + 1) * DEEP, :] = jnp.where(
                    left, turn(east, -start), turn(west, LANES - width - start)
                )


def pack_ocean(ocean, wind, side):
    lanes = lane_ids(ROWS)
    east = jnp.zeros((ROWS, LANES), F32)
    west = jnp.zeros((ROWS, LANES), F32)
    for k in range(8):
        w, part = (k % 4) // 2, k % 2
        if k < 4:
            field = ocean[w, part, 2 * ROWS : 3 * ROWS, :]
        else:
            field = wind[w, part, DEEP : DEEP + ROWS, :]
        start = DEEP * k
        here = (lanes >= start) & (lanes < start + DEEP)
        east = jnp.where(here, turn(field[:, LANES:].astype(F32), start + DEEP), east)
        west = jnp.where(here, turn(field[:, :LANES].astype(F32), start), west)
    side[0] = east.astype(BF16)
    side[1] = west.astype(BF16)


def spread(tiles, first, last):
    ahead = [turn(t, -1) for t in tiles]
    behind = [turn(t, 1) for t in tiles]
    return [
        jnp.where(last, ahead[(c + 1) % 3], ahead[c]) - jnp.where(first, behind[(c + 2) % 3], behind[c])
        for c in range(3)
    ]


def stress_rows(ext, rows_list, bulk, mass, first, last):
    results = []
    for row in rows_list:

        def at(field, shift):
            return [ext[field][c, pl.ds(row + shift, 8), :] for c in range(3)]

        du = spread(at(U, 0), first, last)
        dv = spread(at(V, 0), first, last)
        un, us, vn, vs = at(U, 1), at(U, -1), at(V, 1), at(V, -1)
        bs, es, xs, ys, ss = at(bulk, 0), at(mass, 0), at(X, 0), at(Y, 0), at(S, 0)
        for c in range(3):
            up = vn[c] - vs[c]
            shear = (un[c] - us[c]) + dv[c]
            div = du[c] + up
            ten = du[c] - up
            rate = lax.rsqrt(div * div + 0.25 * (ten * ten + shear * shear) + 1.0)
            keep = jnp.where(es[c] > 0.0, 2.0 / 3.0, 0.0)
            br = bs[c] * rate
            quarter = 0.25 * br
            press = br * div - bs[c]
            pull = quarter * ten
            common = keep * xs[c] + press
            other = keep * ys[c] + press
            results.append((row, c, common + pull, other - pull, keep * ss[c] + quarter * shear))
    for row, c, x, y, s in results:
        rows = pl.ds(row, 8)
        ext[X][c, rows, :] = x
        ext[Y][c, rows, :] = y
        ext[S][c, rows, :] = s


def velocity_rows(ext, rows_list, mass, gx, gy, first, last):
    results = []
    for row in rows_list:

        def at(field, shift):
            return [ext[field][c, pl.ds(row + shift, 8), :] for c in range(3)]

        dx = spread(at(X, 0), first, last)
        ds = spread(at(S, 0), first, last)
        yn, ys, sn, ss = at(Y, 1), at(Y, -1), at(S, 1), at(S, -1)
        es, us, vs, gxs, gys = at(mass, 0), at(U, 0), at(V, 0), at(gx, 0), at(gy, 0)
        for c in range(3):
            e = es[c]
            keep = jnp.where(e > 0.0, 1.0 - e, 0.0)
            fx = dx[c] + (sn[c] - ss[c])
            fy = ds[c] + (yn[c] - ys[c])
            results.append((row, c, keep * us[c] + (gxs[c] + e * fx), keep * vs[c] + (gys[c] + e * fy)))
    for row, c, u, v in results:
        rows = pl.ds(row, 8)
        ext[U][c, rows, :] = u
        ext[V][c, rows, :] = v


def tiles_within(reach):
    above = (reach + 7) // 8
    return BASE // 8 - above, BASE // 8 + ROWS // 8 + above


def sweep(low, high, body):
    for start in range(low, high, GROUP):
        body([8 * tile for tile in range(start, min(start + GROUP, high))])


def kernel(
    vel_hbm,
    str_hbm,
    thk_hbm,
    con_hbm,
    land_hbm,
    cov_hbm,
    oce_hbm,
    win_hbm,
    reg_hbm,
    off_hbm,
    vel_out,
    str_out,
    thk_out,
    vel,
    stress,
    thk,
    con,
    land,
    cov,
    oce,
    win,
    reg,
    off,
    u_ref,
    v_ref,
    x_ref,
    y_ref,
    s_ref,
    b0_ref,
    e0_ref,
    b1_ref,
    e1_ref,
    gx0_ref,
    gy0_ref,
    gx1_ref,
    gy1_ref,
    rim_out,
    edge_out,
    rim_in,
    edge_in,
    side_out,
    side_in,
    mix_out,
    mix_in,
    mix,
    load_sem,
    send_a,
    recv_a,
    send_o,
    recv_o,
    send_s,
    recv_s,
    send_m,
    recv_m,
):
    ext = (u_ref, v_ref, x_ref, y_ref, s_ref, b0_ref, e0_ref, b1_ref, e1_ref, gx0_ref, gy0_ref, gx1_ref, gy1_ref)
    lat, lon = lax.axis_index("lat"), lax.axis_index("lon")
    lats, lons = lax.axis_size("lat"), lax.axis_size("lon")

    def place(up, right):
        return lax.rem(lat + lats + up, lats), lax.rem(lon + lons + right, lons)

    def send_to(up, right, source, target, send, recv):
        to_lat, to_lon = place(up, right)
        return up, pltpu.make_async_remote_copy(
            src_ref=source,
            dst_ref=target,
            send_sem=send,
            recv_sem=recv,
            device_id={"lat": to_lat, "lon": to_lon},
            device_id_type=MESH,
        )

    def begin(copies):
        for up, copy in copies:
            only_if(up, copy.start)

    def arrive(copies):
        for up, copy in copies:
            only_if(-up, copy.wait_recv)

    def leave(copies):
        for up, copy in copies:
            only_if(up, copy.wait_send)

    def exists(up):
        return lat + up < lats if up > 0 else lat + up >= 0

    def only_if(up, act):
        if up:
            pl.when(exists(up))(act)
        else:
            act()

    barrier = pltpu.get_barrier_semaphore()
    greeted = jnp.int32(2)
    for up in NEAR:

        def greet(up=up):
            for right in (-1, 0, 1):
                if up or right:
                    to_lat, to_lon = place(up, right)
                    pl.semaphore_signal(barrier, inc=1, device_id={"lat": to_lat, "lon": to_lon}, device_id_type=MESH)

        only_if(up, greet)
        if up:
            greeted = greeted + jnp.where(exists(up), 3, 0)

    own = pl.ds(2 * ROWS, ROWS)
    loads = [
        pltpu.make_async_copy(source, target, load_sem.at[i])
        for i, (source, target) in enumerate(
            (
                (oce_hbm, oce.at[:, :, own, :]),
                (win_hbm, win.at[:, :, pl.ds(DEEP, ROWS), :]),
                (reg_hbm, reg),
                (off_hbm, off),
                (thk_hbm, thk),
                (con_hbm, con),
                (land_hbm, land),
                (cov_hbm, cov),
                (vel_hbm, vel),
                (str_hbm, stress),
            )
        )
    ]
    for load in loads:
        load.start()

    tail, head = pl.ds(ROWS - DEEP, DEEP), pl.ds(0, DEEP)
    ocean = [
        [
            send_to(
                up,
                0,
                oce_hbm.at[w],
                oce.at[w, :, pl.ds((2 - up) * ROWS, ROWS), :],
                send_o.at[4 * w + i],
                recv_o.at[4 * w + i],
            )
            for i, up in enumerate((2, -2))
        ]
        for w in range(2)
    ]
    stride = 1 - 2 * lax.rem(lat, 2)
    given = pl.ds(pl.multiple_of((2 - stride) * ROWS, ROWS), ROWS)
    taken = pl.ds(pl.multiple_of((2 + stride) * ROWS, ROWS), ROWS)
    pairs = [
        send_to(stride, 0, oce_hbm.at[w], oce.at[w, :, given, :], send_o.at[4 * w + 2], recv_o.at[4 * w + 2])[1]
        for w in range(2)
    ]
    relays = [
        send_to(2 * stride, 0, oce.at[w, :, taken, :], oce.at[w, :, given, :], send_o.at[4 * w + 3], recv_o.at[4 * w + 3])[1]
        for w in range(2)
    ]
    passes_on = (lat + 2 * stride >= 0) & (lat + 2 * stride < lats)
    is_passed = (lat - 2 * stride >= 0) & (lat - 2 * stride < lats)
    winds = [
        send_to(1, 0, win_hbm.at[:, :, tail, :], win.at[:, :, pl.ds(0, DEEP), :], send_m.at[0], recv_m.at[0]),
        send_to(-1, 0, win_hbm.at[:, :, head, :], win.at[:, :, pl.ds(DEEP + ROWS, DEEP), :], send_m.at[1], recv_m.at[1]),
    ]
    mixes = [
        send_to(1, 0, mix_out.at[tail], mix_in.at[0], send_m.at[2], recv_m.at[2]),
        send_to(-1, 0, mix_out.at[head], mix_in.at[1], send_m.at[3], recv_m.at[3]),
    ]
    sides = [
        send_to(
            up,
            right,
            side_out.at[0 if right > 0 else 1],
            side_in.at[0 if right > 0 else 1, pl.ds((2 - up) * ROWS, ROWS), :],
            send_s.at[i],
            recv_s.at[i],
        )
        for i, (up, right) in enumerate((up, right) for up in NEAR for right in (-1, 1))
    ]
    end, body = pl.ds(ROWS + DEEP, DEEP), pl.ds(DEEP, ROWS)
    halo = [
        send_to(up, right, source, target, send_a.at[i], recv_a.at[i])
        for i, (up, right, source, target) in enumerate(
            (
                (1, 0, rim_out.at[0], rim_in.at[1]),
                (-1, 0, rim_out.at[1], rim_in.at[0]),
                (0, 1, edge_out.at[0], edge_in.at[1, body]),
                (0, -1, edge_out.at[1], edge_in.at[0, body]),
                (1, 1, edge_out.at[0, tail], edge_in.at[1, head]),
                (1, -1, edge_out.at[1, tail], edge_in.at[0, head]),
                (-1, 1, edge_out.at[0, head], edge_in.at[1, end]),
                (-1, -1, edge_out.at[1, head], edge_in.at[0, end]),
            )
        )
    ]

    pl.semaphore_wait(barrier, greeted)
    pairs[0].start()
    begin(ocean[0])
    pairs[1].start()
    begin(ocean[1] + winds)

    def blank(up, parts):
        @pl.when(jnp.logical_not(exists(up)))
        def _():
            for part in parts:
                part[...] = jnp.zeros(part.shape, part.dtype)

    for up, outer, inner_block in ((-1, pl.ds(0, DEEP), 1), (1, pl.ds(DEEP + ROWS, DEEP), 3)):
        beside = pl.ds(inner_block * ROWS, ROWS)
        side = 1 if up < 0 else 0
        blank(up, (rim_in.at[side], edge_in.at[:, outer, :], win.at[:, :, outer, :], mix_in.at[1 - side], oce.at[:, :, beside, :], side_in.at[:, beside, :]))
    for up, block in ((-2, 0), (2, 4)):
        beyond = pl.ds(block * ROWS, ROWS)
        blank(up, (oce.at[:, :, beyond, :], side_in.at[:, beyond, :]))

    for load in loads[:4]:
        load.wait()
    pack_ocean(oce, win, side_out)

    line = lax.broadcasted_iota(jnp.int32, (ROWS, ROWS), 0)
    mark = lax.broadcasted_iota(jnp.int32, (ROWS, ROWS), 1)
    upward = jnp.sum(jnp.where(line == mark, jnp.broadcast_to(off[...], (ROWS, ROWS)), 0), axis=1, keepdims=True) > 0
    upward = jnp.broadcast_to(upward, (ROWS, LANES))
    weights = turn(reg[...].astype(F32), ROWS)
    left = lane_ids(ROWS) < ROWS
    lower = jnp.where(left & upward, 0.0, weights)
    upper = jnp.where(left & upward, weights, 0.0)
    mix_out[:, :LANES] = lower.astype(BF16)
    mix_out[:, LANES:] = upper.astype(BF16)
    lower, upper = turn(lower, ROWS), turn(upper, ROWS)
    inner = slice(DEEP, DEEP + ROWS)
    mix[inner, :LANES] = jnp.where(left, 0.0, lower).astype(BF16)
    mix[inner, LANES : 2 * LANES] = jnp.where(left, lower, upper).astype(BF16)
    mix[inner, 2 * LANES :] = jnp.zeros((ROWS, LANES), BF16)

    for load in loads[4:]:
        load.wait()

    lanes_one = lane_ids(1)[:, : cov.shape[1]]
    flags = [
        jnp.sum(jnp.where(lanes_one == 2 * lon + c, cov[...], 0), axis=1, keepdims=True) > 0 for c in range(2)
    ]

    def prepare(i):
        row = i * 8
        rows = pl.ds(row, 8)
        inside = pl.ds(BASE + row, 8)
        for c in range(2):
            cells = slice(c * LANES, (c + 1) * LANES)
            ext[U][c, inside, :] = vel[0, rows, cells]
            ext[V][c, inside, :] = vel[1, rows, cells]
            one, two = stress[0, rows, cells], stress[1, rows, cells]
            ext[X][c, inside, :] = 0.25 * (one + two)
            ext[Y][c, inside, :] = 0.25 * (one - two)
            ext[S][c, inside, :] = 0.5 * stress[2, rows, cells]
            open_mask = land[rows, cells].astype(F32)
            share = [con[k, rows, cells] for k in range(CATS)]
            thick = [thk[k, rows, cells] for k in range(CATS)]
            area = sum(share[1:], share[0])
            weight = jnp.exp(-2.0 * (1.0 - area)) * open_mask * (1.0 / 12.0)
            volume = sum((share[k] * thick[k] for k in range(1, CATS)), share[0] * thick[0])
            grow = jnp.broadcast_to(flags[c], (8, LANES))
            for bulk, mass in ((B0, E0), (B1, E1)):
                mean = volume / area
                thick = [jnp.where(grow, t + 0.3 / (0.5 + t) + 0.3 * (mean - t), t) for t in thick]
                volume = sum((share[k] * thick[k] for k in range(1, CATS)), share[0] * thick[0])
                ext[bulk][c, inside, :] = volume * weight
                ext[mass][c, inside, :] = 0.5 * open_mask / (volume + 1.0)
            for k in range(CATS):
                thk_out[k, rows, cells] = thick[k]

    for i in range(ROWS // 8):
        prepare(i)

    pack_sides(ext, rim_out, edge_out)
    begin(halo + mixes + sides)
    for pair, relay in zip(pairs, relays):
        pair.wait_recv()
        pl.when(passes_on)(relay.start)

    lanes = lane_ids(8)
    first, last = lanes == 0, lanes == LANES - 1
    band = slice(PAD, PAD + WIDE)

    def force(w, mass, fields):
        for part, field in enumerate(fields):
            current = jnp.dot(mix[:, : 5 * ROWS], oce[w, part], preferred_element_type=F32)
            total = current + win[w, part].astype(F32)
            for c in range(2):
                ext[field][c, band, :] = ext[mass][c, band, :] * total[:, c * LANES : (c + 1) * LANES]

    arrive(halo)
    unpack_sides(ext, rim_in, edge_in)

    reach = DEEP
    for bulk, mass, gx, gy in ((B0, E0, GX0, GY0), (B1, E1, GX1, GY1)):
        for step in range(SUB):
            low, high = tiles_within(reach - 1)
            sweep(low, high, lambda rows: stress_rows(ext, rows, bulk, mass, first, last))
            if step == 0 and bulk == B0:
                arrive(mixes)
                mix[:DEEP, : 2 * LANES] = mix_in[0]
                mix[:DEEP, 2 * LANES :] = jnp.zeros((DEEP, LANES), BF16)
                mix[DEEP + ROWS :, :LANES] = jnp.zeros((DEEP, LANES), BF16)
                mix[DEEP + ROWS :, LANES:] = mix_in[1]
                arrive(sides)
                near = slice(2 * ROWS - DEEP, 3 * ROWS + DEEP)
                flows = [
                    jnp.dot(mix[:, : 5 * ROWS], side_in[d], preferred_element_type=F32)
                    + turn(side_in[d, near, :].astype(F32), ROWS)
                    for d in range(2)
                ]
                is_east = lane_ids(WIDE) < LANES // 2
                for k, (field, weight) in enumerate(((GX0, E0), (GY0, E0), (GX1, E1), (GY1, E1))):
                    total = jnp.where(is_east, turn(flows[1], -DEEP * k), turn(flows[0], LANES - DEEP - DEEP * k))
                    ext[field][2, band, :] = ext[weight][2, band, :] * total
                arrive(winds + ocean[0])
                pl.when(is_passed)(relays[0].wait_recv)
                force(0, E0, (GX0, GY0))
            if step == 0 and bulk == B1:
                arrive(ocean[1])
                pl.when(is_passed)(relays[1].wait_recv)
                force(1, E1, (GX1, GY1))
            low, high = tiles_within(reach - 2)
            sweep(low, high, lambda rows: velocity_rows(ext, rows, mass, gx, gy, first, last))
            reach -= 2

    inner = slice(BASE, BASE + ROWS)
    for c in range(2):
        cells = slice(c * LANES, (c + 1) * LANES)
        one, two = ext[X][c, inner, :], ext[Y][c, inner, :]
        str_out[0, :, cells] = 2.0 * (one + two)
        str_out[1, :, cells] = 2.0 * (one - two)
        str_out[2, :, cells] = 2.0 * ext[S][c, inner, :]
        vel_out[0, :, cells] = ext[U][c, inner, :]
        vel_out[1, :, cells] = ext[V][c, inner, :]

    leave(ocean[0] + ocean[1] + winds + mixes + sides + halo)
    for pair, relay in zip(pairs, relays):
        pair.wait_send()
        pl.when(passes_on)(relay.wait_send)


def deliver(vel, stress, thick, vel_out, str_out, thk_out, sems):
    copies = [
        pltpu.make_async_copy(source, target, sems.at[i])
        for i, (source, target) in enumerate(((vel, vel_out), (stress, str_out), (thick, thk_out)))
    ]
    for copy in copies:
        copy.start()
    for copy in copies:
        copy.wait()


def local(velocity, stress, thickness, concentration, land_mask, covered, ocean_current, wind_stress, regrid_weights, tile_offset):
    offsets = tile_offset.reshape(1, -1)
    arrays = (velocity, stress, thickness, concentration, land_mask, covered, ocean_current, wind_stress, regrid_weights, offsets)
    width = velocity.shape[-1]
    held = {6: (2, 2, 5 * ROWS, width), 7: (2, 2, WIDE, width)}
    staged = [pltpu.VMEM(held.get(i, a.shape), a.dtype) for i, a in enumerate(arrays)]
    field = pltpu.VMEM((3, TALL, LANES), F32)
    rim = pltpu.VMEM((2, len(STATE), 2, DEEP, LANES), BF16)
    dma = pltpu.SemaphoreType.DMA
    results = pl.pallas_call(
        kernel,
        out_shape=[pltpu.VMEM(a.shape, F32) for a in (velocity, stress, thickness)],
        in_specs=[pl.BlockSpec(memory_space=pl.ANY)] * len(arrays),
        out_specs=[pl.BlockSpec(memory_space=pltpu.VMEM)] * 3,
        scratch_shapes=staged
        + [field] * 13
        + [
            rim,
            pltpu.VMEM((2, ROWS, LANES), BF16),
            rim,
            pltpu.VMEM((2, WIDE, LANES), BF16),
            pltpu.VMEM((2, ROWS, LANES), BF16),
            pltpu.VMEM((2, 5 * ROWS, LANES), BF16),
            pltpu.VMEM((ROWS, 2 * LANES), BF16),
            pltpu.VMEM((2, DEEP, 2 * LANES), BF16),
            pltpu.VMEM((WIDE, 3 * LANES), BF16),
        ]
        + [dma((n,)) for n in (10, 8, 8, 8, 8, 10, 10, 4, 4)],
        compiler_params=pltpu.CompilerParams(collective_id=0, has_side_effects=True),
    )(*arrays)

    return pl.pallas_call(
        deliver,
        out_shape=[jax.ShapeDtypeStruct(a.shape, F32) for a in (velocity, stress, thickness)],
        in_specs=[pl.BlockSpec(memory_space=pltpu.VMEM)] * 3,
        out_specs=[pl.BlockSpec(memory_space=pl.ANY)] * 3,
        scratch_shapes=[dma((3,))],
    )(*[pltpu.with_memory_space_constraint(r, pltpu.VMEM) for r in results])


def solution(mesh):
    return jax.shard_map(
        local,
        mesh=mesh,
        in_specs=(
            P(None, "lat", "lon"),
            P(None, "lat", "lon"),
            P(None, "lat", "lon"),
            P(None, "lat", "lon"),
            P("lat", "lon"),
            P("lat", None),
            P(None, None, "lat", "lon"),
            P(None, None, "lat", "lon"),
            P("lat", None),
            P("lat"),
        ),
        out_specs=(P(None, "lat", "lon"), P(None, "lat", "lon"), P(None, "lat", "lon")),
        check_vma=False,
    )
```
